32 devices in a mesh: slab: 4 (over x, core), grp: 8 (over z, y).
Axes of the slice: x: 2, y: 2, z: 4, core: 2. Of those that a mesh axis runs over, the one named last changes fastest.
Arguments:
- raw_frames: bfloat16 [256, 48, 10752], P('grp', 'slab'), may hold values from -700 to 700
- mask_index: int32 [57344], P(('slab', 'grp')), may hold values from 0 to 516095, as said below
- subspace: bfloat16 [1200, 57344], P(None, ('slab', 'grp')), may hold values from -6 to 6
- rotation: bfloat16 [1456, 1200], replicated, may hold values from -0.15625 to 0.15625
Outputs:
- gram: float32 [1456, 1456], P('grp')
- new_subspace: bfloat16 [1200, 57344], P(None, ('slab', 'grp'))
The draws below stay inside these ranges and needn't reach their ends.
Inputs may be any that keep to these rules, and one draw needn't show every extreme that they name: `mask_index`: entries are distinct flat grid positions that come in runs of 128 consecutive positions, each run starting at a multiple of 128; the 14336 entries of aligned block s lie in z planes s * 12 to (s + 1) * 12 - 1 and rise within the block; the first 3584 of a block lie in its lowest 3 planes, the last 3584 in its highest 3 planes, the others in the planes between.
All inputs are finite; a program needn't handle non-finite values.
Results may differ from the reference program's by a relative error of at most 0.006.
Values may be sent and summed in bfloat16 or wider, within the bound.
A program may use at most 192 MiB of HBM per device.

```python
import math
import jax
import jax.numpy as jnp
from jax import lax

NX = 96
NYX = 10752
RUN = 128
CZ = 12
NZ = 48
RAD = 3
FRAMES = 256
K = 1200
KX = 1456
MV_DEV = 1792
MASKED = 57344
SLAB_ROWS = 14336
RIM_ROWS = 3584


def pick_runs(run_key, run_total, run_count, first_cell):
    chosen = jnp.sort(jax.random.permutation(run_key, run_total)[:run_count]).astype(jnp.int32)
    within = jnp.arange(RUN, dtype=jnp.int32)
    return (chosen[:, None] * RUN + within[None, :]).reshape(-1) + first_cell


def draw_mask_index(key, part):
    slab_count = NZ // CZ
    slab_cells = CZ * NYX
    rim_runs = RAD * NYX // RUN
    middle_runs = (CZ - 2 * RAD) * NYX // RUN
    middle_rows = SLAB_ROWS - 2 * RIM_ROWS

    def per_slab(slab_number):
        slab_key = jax.random.fold_in(key, slab_number)
        lower = pick_runs(jax.random.fold_in(slab_key, 1), rim_runs, RIM_ROWS // RUN, 0)
        upper = pick_runs(jax.random.fold_in(slab_key, 2), rim_runs, RIM_ROWS // RUN, (CZ - RAD) * NYX)
        pieces = [lower]
        if middle_rows > 0:
            pieces.append(pick_runs(jax.random.fold_in(slab_key, 3), middle_runs, middle_rows // RUN, RAD * NYX))
        pieces.append(upper)
        return jnp.concatenate(pieces) + slab_number * slab_cells
    return jax.vmap(per_slab)(jnp.arange(slab_count, dtype=jnp.int32)).reshape(-1).astype(jnp.int32)


def draw_raw_frames(key, part):
    noise_key = jax.random.fold_in(key, 11)
    rough_key = jax.random.fold_in(key, 12)
    depth = jnp.arange(NZ, dtype=jnp.float32) / max(NZ - 1, 1)
    base = jax.random.truncated_normal(noise_key, -4.0, 4.0, (FRAMES, NZ, NYX), jnp.float32)
    depth_scale = jnp.exp(jnp.log(10.0) * depth)
    frame_scale = jnp.exp(jnp.log(3.0) * jnp.arange(FRAMES, dtype=jnp.float32) / max(FRAMES - 1, 1))
    rough = jnp.exp(jax.random.uniform(rough_key, (1, NZ, NYX), jnp.float32, -0.7, 0.7))
    values = base * rough * depth_scale[None, :, None] * frame_scale[:, None, None]
    return values.astype(jnp.bfloat16)


def spiked(result, own_key, source, target, parts, factor):
    owner, partner = [(jnp.arange(result.shape[position]) // (result.shape[position] // parts)).reshape([-1 if axis == position else 1 for axis in range(result.ndim)]) for position in (source, target)]
    chosen = jax.random.permutation(own_key, parts)[partner]
    strong = (owner == chosen) | (owner == (partner + parts // 2) % parts)
    return jnp.where(strong, factor * result, result)


def levels(rng, dims, cuts, smallest, top_value):
    def one(axis_at, blocks):
        steps = jax.random.uniform(jax.random.fold_in(jax.random.fold_in(rng, 6), axis_at), (blocks,), jnp.float32, smallest / len(cuts), top_value / len(cuts))
        return jnp.repeat(jnp.exp(steps), dims[axis_at] // blocks).reshape((-1,) + (1,) * (len(dims) - axis_at - 1))

    gain = one(*cuts[0])
    for cut in cuts[1:]:
        gain = gain * one(*cut)
    return gain


def centred(key, dims, scale, most, split=(), held_as=jnp.bfloat16):
    factor_of = levels(key, dims, split, -0.22, 0.18) if split else 1.0
    entries = jax.random.normal(key, dims, jnp.float32) * scale * factor_of
    return jnp.minimum(jnp.maximum(entries, -most), most).astype(held_as)


def bell_draw_with(key, shape, deviation, most, shards, heavy, kind=jnp.bfloat16):
    drawn = deviation * jax.random.normal(key, shape, jnp.float32)
    if shards:
        drawn = drawn * levels(key, shape, shards, -0.22, 0.18)
    return jnp.clip(spiked(drawn, jax.random.fold_in(key, 3), *heavy), -most, most).astype(kind)


def setup_inputs(seed: int = 0) -> dict:
    splits = jax.random.split(jax.random.key(seed), 5)
    return {
        "raw_frames": draw_raw_frames(jax.random.fold_in(splits[4], 71), 0),
        "mask_index": draw_mask_index(jax.random.fold_in(splits[4], 71), 0),
        "subspace": bell_draw_with(splits[2], (K, MASKED), 1.0, 6.0, ((1, 32),), (1, 0, 16, 2.0)),
        "rotation": centred(splits[3], (KX, K), KX ** -0.5, 0.15625),
    }


smooth_sigma = 1.0617
epsilon = 1e-06

def tap_weights():
    unscaled = [math.exp(-offset * offset / (2.0 * smooth_sigma * smooth_sigma)) for offset in range(-RAD, RAD + 1)]
    summed = sum(unscaled)
    return [weight / summed for weight in unscaled]

def along_rows(volume):
    weights = tap_weights()
    extent = volume.shape[-1]
    column = lax.broadcasted_iota(jnp.int32, (extent,), 0) % NX
    padded = jnp.pad(volume, [(0, 0)] * (volume.ndim - 1) + [(RAD, RAD)])
    summed = jnp.zeros(volume.shape, jnp.float32)
    for offset in range(-RAD, RAD + 1):
        shifted = lax.slice_in_dim(padded, RAD + offset, RAD + offset + extent, axis=volume.ndim - 1)
        inside = (column + offset >= 0) & (column + offset < NX)
        summed = summed + weights[offset + RAD] * jnp.where(inside, shifted, 0.0)
    return summed

def along_columns(volume):
    weights = tap_weights()
    extent = volume.shape[-1]
    reach_cells = RAD * NX
    padded = jnp.pad(volume, [(0, 0)] * (volume.ndim - 1) + [(reach_cells, reach_cells)])
    summed = jnp.zeros(volume.shape, jnp.float32)
    for offset in range(-RAD, RAD + 1):
        begin = reach_cells + offset * NX
        shifted = lax.slice_in_dim(padded, begin, begin + extent, axis=volume.ndim - 1)
        summed = summed + weights[offset + RAD] * shifted
    return summed

def along_depth(padded, slab_depth):
    weights = tap_weights()
    summed = None
    for offset in range(-RAD, RAD + 1):
        shifted = lax.slice_in_dim(padded, RAD + offset, RAD + offset + slab_depth, axis=padded.ndim - 2)
        term = weights[offset + RAD] * shifted
        summed = term if summed is None else summed + term
    return summed

def reference(raw_frames, mask_index, subspace, rotation):

    def one_frame(frame_data):
        planar = along_columns(along_rows(frame_data.astype(jnp.float32)))
        padded = jnp.pad(planar, [(RAD, RAD), (0, 0)])
        volume = along_depth(padded, NZ).reshape(-1)
        return jnp.take(volume, mask_index, axis=0).astype(jnp.bfloat16)
    smoothed = lax.map(one_frame, raw_frames)
    subject_frames = FRAMES // 2
    halves = smoothed.astype(jnp.float32).reshape(2, subject_frames, MASKED)
    centered = (halves - lax.optimization_barrier(jnp.mean(halves, axis=1, keepdims=True))).astype(jnp.bfloat16)
    widened = centered.astype(jnp.float32)
    power = lax.optimization_barrier(jnp.sum(widened * widened, axis=(1, 2)))
    scales = lax.rsqrt(power / (MASKED * subject_frames) + epsilon)
    centered = centered.reshape(FRAMES, MASKED)
    row_scale = jnp.concatenate([jnp.ones((K,), jnp.float32), jnp.repeat(scales, subject_frames)])
    rotation_wide = rotation.astype(jnp.float32)
    basis_rot = rotation_wide[:K]
    first_rot = rotation_wide[K:K + subject_frames]
    second_rot = rotation_wide[K + subject_frames:]
    highest = lax.Precision.HIGHEST
    block_count = MASKED // MV_DEV

    def accumulate(gram_raw, block_index):
        first_col = (block_index * MV_DEV).astype(jnp.int32)
        basis_cols = lax.dynamic_slice_in_dim(subspace, first_col, MV_DEV, 1).astype(jnp.float32)
        data_cols = lax.dynamic_slice_in_dim(centered, first_col, MV_DEV, 1).astype(jnp.float32)
        stacked = jnp.concatenate([basis_cols, data_cols], 0)
        gram_raw = gram_raw + jnp.dot(stacked, stacked.T, precision=highest)
        from_basis = jnp.dot(basis_rot.T, basis_cols, precision=highest)
        from_first = jnp.dot(first_rot.T, data_cols[:subject_frames], precision=highest)
        from_second = jnp.dot(second_rot.T, data_cols[subject_frames:], precision=highest)
        row_block = (from_basis + scales[0] * from_first + scales[1] * from_second).astype(jnp.bfloat16)
        return (gram_raw, row_block)
    gram_raw, pieces = lax.scan(accumulate, jnp.zeros((KX, KX), jnp.float32), jnp.arange(block_count, dtype=jnp.int32))
    new_subspace = jnp.transpose(pieces, (1, 0, 2)).reshape(K, MASKED)
    gram = gram_raw * (row_scale[:, None] * row_scale[None, :]) / MASKED
    return (gram, new_subspace)
```

```python
import functools
import math

import jax
import jax.numpy as jnp
import numpy as np
from jax import lax
from jax.experimental import pallas as pl
from jax.experimental.pallas import tpu as pltpu
from jax.sharding import PartitionSpec as P

NX = 96
RUN = 128
RAD = 3
K = 1200
MESH = pl.DeviceIdType.MESH

smooth_sigma = 1.0617
epsilon = 1e-06

WIDE = 2 * RUN
LEFT = 3 * RUN
SPAN = 8 * RUN


def tap_weights():
    unscaled = [
        math.exp(-offset * offset / (2.0 * smooth_sigma * smooth_sigma))
        for offset in range(-RAD, RAD + 1)
    ]
    summed = sum(unscaled)
    return [weight / summed for weight in unscaled]


def plane_weights():
    taps = np.array(tap_weights())
    kinds = NX // math.gcd(WIDE, NX)
    out = np.zeros((kinds, SPAN, WIDE))
    for kind in range(kinds):
        target = np.arange(WIDE)
        column = (kind * WIDE + target) % NX
        for dy in range(-RAD, RAD + 1):
            for dx in range(-RAD, RAD + 1):
                inside = (column + dx >= 0) & (column + dx < NX)
                source = target + LEFT + dy * NX + dx
                out[kind, source[inside], target[inside]] = taps[dy + RAD] * taps[dx + RAD]
    return out.astype(jnp.bfloat16)


def exchange_kernel(total, groups, summed, x_ref, out_ref, landed, send_sem, recv_sem):
    me = lax.axis_index("slab") * groups + lax.axis_index("grp")
    barrier = pltpu.get_barrier_semaphore()

    def place(peer):
        return (peer // groups, lax.rem(peer, groups))

    def greet(step, _):
        pl.semaphore_signal(
            barrier, inc=1, device_id=place(lax.rem(me + step, total)), device_id_type=MESH
        )
        return 0

    lax.fori_loop(1, total, greet, 0)
    pl.semaphore_wait(barrier, total - 1)

    def copy(step):
        return pltpu.make_async_remote_copy(
            src_ref=x_ref,
            dst_ref=landed.at[step],
            send_sem=send_sem.at[step],
            recv_sem=recv_sem.at[step],
            device_id=place(lax.rem(me + step, total)),
            device_id_type=MESH,
        )

    def start(step, _):
        copy(step).start()
        return 0

    def finish(step, _):
        copy(step).wait()
        return 0

    lax.fori_loop(1, total, start, 0)
    landed[0] = x_ref[...]
    lax.fori_loop(1, total, finish, 0)
    if summed:
        out_ref[...] = jnp.sum(landed[...], axis=0)
    else:
        def put(step, _):
            out_ref[lax.rem(me + total - step, total)] = landed[step]
            return 0

        lax.fori_loop(0, total, put, 0)


def exchange(x, summed, collective_id):
    groups = lax.axis_size("grp")
    total = groups * lax.axis_size("slab")
    shape = x.shape if summed else (total,) + x.shape
    return pl.pallas_call(
        functools.partial(exchange_kernel, total, groups, summed),
        out_shape=jax.ShapeDtypeStruct(shape, x.dtype),
        in_specs=[pl.BlockSpec(memory_space=pltpu.VMEM)],
        out_specs=pl.BlockSpec(memory_space=pltpu.VMEM),
        scratch_shapes=[
            pltpu.VMEM((total,) + x.shape, x.dtype),
            pltpu.SemaphoreType.DMA((total,)),
            pltpu.SemaphoreType.DMA((total,)),
        ],
        compiler_params=pltpu.CompilerParams(
            collective_id=collective_id, has_side_effects=True
        ),
    )(x)


def smooth_kernel(depth, frames, own, up, z_ref, r_ref, x_ref, w_ref, own_ref, up_ref, down_ref, y_ref):
    taps = tap_weights()
    kinds = w_ref.shape[0]
    steps = y_ref.shape[0] // (2 * kinds)

    def planar(step, _):
        for kind in range(kinds):
            place = step * kinds + kind
            begin = pl.multiple_of(place * WIDE, WIDE)
            found = jnp.dot(
                x_ref[:, pl.ds(begin, SPAN)], w_ref[kind], preferred_element_type=jnp.float32
            )
            y_ref[2 * place] = found[:, :RUN]
            y_ref[2 * place + 1] = found[:, RUN:]
        return 0

    lax.fori_loop(0, steps, planar, 0)

    def picked(run):
        z = z_ref[run]
        r = r_ref[run]
        total = None
        for offset in range(-RAD, RAD + 1):
            at = z + offset
            weight = jnp.where((at >= 0) & (at < depth), jnp.float32(taps[offset + RAD]), 0.0)
            row = pl.multiple_of(jnp.clip(at, 0, depth - 1) * frames, frames)
            term = weight * y_ref[r, pl.ds(row, frames), :]
            total = term if total is None else total + term
        return total

    def put(ref, first):
        def one(run, _):
            ref[run] = picked(run + first).astype(ref.dtype)
            return 0

        lax.fori_loop(0, ref.shape[0], one, 0)

    put(up_ref, own)
    put(down_ref, own + up)
    put(own_ref, 0)


def smooth(cells, weights, planes_at, runs_at, depth, frames, extent, own, rim):
    vmem = pl.BlockSpec(memory_space=pltpu.VMEM)
    smem = pl.BlockSpec(memory_space=pltpu.SMEM)
    return pl.pallas_call(
        functools.partial(smooth_kernel, depth, frames, own, rim),
        out_shape=(
            jax.ShapeDtypeStruct((own, frames, RUN), jnp.float32),
            jax.ShapeDtypeStruct((rim, frames, RUN), jnp.bfloat16),
            jax.ShapeDtypeStruct((rim, frames, RUN), jnp.bfloat16),
        ),
        in_specs=[smem, smem, vmem, vmem],
        out_specs=(vmem, vmem, vmem),
        scratch_shapes=[pltpu.VMEM((extent // RUN, depth * frames, RUN), jnp.float32)],
        compiler_params=pltpu.CompilerParams(vmem_limit_bytes=48 * 1024 * 1024),
    )(planes_at, runs_at, cells, weights)


def body(raw_frames, mask_index, subspace, rotation):
    frames_here, slab_depth, extent = raw_frames.shape
    per_device = subspace.shape[1]
    group_count = lax.axis_size("grp")
    slab_count = lax.axis_size("slab")
    masked = per_device * slab_count * group_count
    frame_count = frames_here * group_count
    subject_frames = frame_count // 2
    order_rows = K + frame_count
    rows_here = order_rows // group_count
    first_row = lax.axis_index("grp") * rows_here
    slab = lax.axis_index("slab")
    runs_here = per_device // RUN
    own = runs_here * group_count
    rim = own * RAD // slab_depth
    both = ("slab", "grp")

    basis_part = lax.dot_general(
        subspace, subspace, (((1,), (1,)), ((), ())), preferred_element_type=jnp.float32
    ).astype(jnp.bfloat16)
    basis_rows = lax.psum_scatter(
        jnp.pad(basis_part, ((0, frame_count), (0, 0))), "grp", scatter_dimension=0, tiled=True
    )
    basis_rows = lax.psum(basis_rows.astype(jnp.float32), "slab")

    starts = exchange(mask_index.reshape(runs_here, RUN), False, 1)[:, :, 0]
    starts = starts.reshape(slab_count, own) - slab * (slab_depth * extent)
    wanted = jnp.concatenate(
        [
            lax.dynamic_index_in_dim(starts, slab, 0, False),
            lax.dynamic_index_in_dim(starts, jnp.minimum(slab + 1, slab_count - 1), 0, False)[:rim],
            lax.dynamic_index_in_dim(starts, jnp.maximum(slab - 1, 0), 0, False)[own - rim :],
        ]
    )
    planes_at = jnp.floor_divide(wanted, extent)
    runs_at = (wanted - planes_at * extent) // RUN

    cells = jnp.pad(
        raw_frames.transpose(1, 0, 2), ((0, 0), (0, 0), (LEFT, SPAN - WIDE - LEFT))
    ).reshape(slab_depth * frames_here, -1)
    inner, upward, downward = smooth(
        cells, jnp.asarray(plane_weights()), planes_at, runs_at,
        slab_depth, frames_here, extent, own, rim,
    )
    ends = slab_count - 1
    from_below = lax.ppermute(upward, "slab", [(i, i + 1) for i in range(ends)])
    from_above = lax.ppermute(downward, "slab", [(i + 1, i) for i in range(ends)])
    smoothed = jnp.concatenate(
        [
            inner[:rim] + from_below.astype(jnp.float32),
            inner[rim : own - rim],
            inner[own - rim :] + from_above.astype(jnp.float32),
        ]
    ).astype(jnp.bfloat16)
    regrouped = lax.all_to_all(smoothed, "grp", split_axis=0, concat_axis=0, tiled=True)
    halves = (
        regrouped.reshape(group_count, runs_here, frames_here, RUN)
        .transpose(0, 2, 1, 3)
        .reshape(2, subject_frames, per_device)
        .astype(jnp.float32)
    )
    centered = (halves - jnp.mean(halves, axis=1, keepdims=True)).astype(jnp.bfloat16)
    widened = centered.astype(jnp.float32)
    squares = jnp.sum(widened * widened, axis=(1, 2))
    power = exchange(jnp.broadcast_to(jnp.pad(squares, (0, 6))[:, None], (8, RUN)), True, 2)[:2, 0]
    centered = centered.reshape(frame_count, per_device)
    stacked = jnp.concatenate([subspace, centered], 0)
    data_part = lax.psum(
        lax.dot_general(
            stacked, centered, (((1,), (1,)), ((), ())), preferred_element_type=jnp.float32
        ),
        both,
    )
    scales = lax.rsqrt(power / (masked * subject_frames) + epsilon)
    row_scale = jnp.concatenate([jnp.ones((K,), jnp.float32), jnp.repeat(scales, subject_frames)])

    turned = (rotation.astype(jnp.float32) * row_scale[:, None]).astype(jnp.bfloat16)
    new_subspace = lax.dot_general(
        turned, stacked, (((0,), (0,)), ((), ())), preferred_element_type=jnp.float32
    ).astype(jnp.bfloat16)

    right = lax.dynamic_slice_in_dim(data_part, first_row, rows_here, 0)
    low = jnp.pad(data_part[:K].T, ((rows_here, rows_here), (0, 0)))
    low = lax.dynamic_slice_in_dim(low, jnp.maximum(first_row - K + rows_here, 0), rows_here, 0)
    owned = jnp.concatenate([basis_rows + low, right], 1)
    owned_scale = lax.dynamic_slice_in_dim(row_scale, first_row, rows_here, 0)
    gram_rows = owned * (owned_scale[:, None] * row_scale[None, :]) / masked
    return (gram_rows, new_subspace)


def solution(mesh):
    placed = (P("grp", "slab", None), P(("slab", "grp")), P(None, ("slab", "grp")), P())
    return jax.shard_map(
        body,
        mesh=mesh,
        in_specs=placed,
        out_specs=(P("grp", None), P(None, ("slab", "grp"))),
        check_vma=False,
    )
```

```python
import functools
import math

import jax
import jax.numpy as jnp
import numpy as np
from jax import lax
from jax.experimental import pallas as pl
from jax.experimental.pallas import tpu as pltpu
from jax.sharding import PartitionSpec as P

NX = 96
RUN = 128
RAD = 3
K = 1200
MESH = pl.DeviceIdType.MESH

smooth_sigma = 1.0617
epsilon = 1e-06

WIDE = 2 * RUN
LEFT = 3 * RUN
SPAN = 8 * RUN


def tap_weights():
    unscaled = [
        math.exp(-offset * offset / (2.0 * smooth_sigma * smooth_sigma))
        for offset in range(-RAD, RAD + 1)
    ]
    summed = sum(unscaled)
    return [weight / summed for weight in unscaled]


def plane_weights():
    taps = np.array(tap_weights())
    kinds = NX // math.gcd(WIDE, NX)
    out = np.zeros((kinds, SPAN, WIDE))
    for kind in range(kinds):
        target = np.arange(WIDE)
        column = (kind * WIDE + target) % NX
        for dy in range(-RAD, RAD + 1):
            for dx in range(-RAD, RAD + 1):
                inside = (column + dx >= 0) & (column + dx < NX)
                source = target + LEFT + dy * NX + dx
                out[kind, source[inside], target[inside]] = taps[dy + RAD] * taps[dx + RAD]
    return out.astype(jnp.bfloat16)


def exchange_kernel(total, groups, summed, x_ref, out_ref, landed, send_sem, recv_sem):
    me = lax.axis_index("slab") * groups + lax.axis_index("grp")
    barrier = pltpu.get_barrier_semaphore()

    def place(peer):
        return (peer // groups, lax.rem(peer, groups))

    def greet(step, _):
        pl.semaphore_signal(
            barrier, inc=1, device_id=place(lax.rem(me + step, total)), device_id_type=MESH
        )
        return 0

    lax.fori_loop(1, total, greet, 0)
    pl.semaphore_wait(barrier, total - 1)

    def copy(step):
        return pltpu.make_async_remote_copy(
            src_ref=x_ref,
            dst_ref=landed.at[step],
            send_sem=send_sem.at[step],
            recv_sem=recv_sem.at[step],
            device_id=place(lax.rem(me + step, total)),
            device_id_type=MESH,
        )

    def start(step, _):
        copy(step).start()
        return 0

    def finish(step, _):
        copy(step).wait()
        return 0

    lax.fori_loop(1, total, start, 0)
    landed[0] = x_ref[...]
    lax.fori_loop(1, total, finish, 0)
    if summed:
        out_ref[...] = jnp.sum(landed[...], axis=0)
    else:
        def put(step, _):
            out_ref[lax.rem(me + total - step, total)] = landed[step]
            return 0

        lax.fori_loop(0, total, put, 0)


def exchange(x, summed, collective_id):
    groups = lax.axis_size("grp")
    total = groups * lax.axis_size("slab")
    shape = x.shape if summed else (total,) + x.shape
    return pl.pallas_call(
        functools.partial(exchange_kernel, total, groups, summed),
        out_shape=jax.ShapeDtypeStruct(shape, x.dtype),
        in_specs=[pl.BlockSpec(memory_space=pltpu.VMEM)],
        out_specs=pl.BlockSpec(memory_space=pltpu.VMEM),
        scratch_shapes=[
            pltpu.VMEM((total,) + x.shape, x.dtype),
            pltpu.SemaphoreType.DMA((total,)),
            pltpu.SemaphoreType.DMA((total,)),
        ],
        compiler_params=pltpu.CompilerParams(
            collective_id=collective_id, has_side_effects=True
        ),
    )(x)


def axes_of(groups, slabs):
    outer = 4 if groups % 4 == 0 else 1
    cores = 2 if slabs % 2 == 0 else 1
    return outer, groups // outer, slabs // cores, cores


def coordinates(sizes):
    slab, grp = lax.axis_index("slab"), lax.axis_index("grp")
    return [grp // sizes[1], lax.rem(grp, sizes[1]), slab // sizes[3], lax.rem(slab, sizes[3])]


def device_at(at, sizes):
    return (at[2] * sizes[3] + at[3], at[0] * sizes[1] + at[1])


def moved(at, sizes, axis, step):
    other = lax.rem(at[axis] + step, sizes[axis])
    return at[:axis] + [other] + at[axis + 1 :], other


def greet_all(sizes):
    barrier = pltpu.get_barrier_semaphore()
    at = coordinates(sizes)
    count = 0
    for axis, size in enumerate(sizes):
        for step in range(1, size):
            there, _ = moved(at, sizes, axis, step)
            pl.semaphore_signal(
                barrier, inc=1, device_id=device_at(there, sizes), device_id_type=MESH
            )
            count += 1
    return barrier, count


class Scatter:
    def __init__(self, sizes, axis, src, landed, out, sems):
        self.sizes, self.axis, self.src, self.landed, self.out = sizes, axis, src, landed, out
        self.send_sem, self.recv_sem = sems
        self.at = coordinates(sizes)

    def part(self, where):
        return self.src.at[(slice(None),) * self.axis + (where,)]

    def copy(self, step):
        there, other = moved(self.at, self.sizes, self.axis, step)
        return pltpu.make_async_remote_copy(
            src_ref=self.part(other),
            dst_ref=self.landed.at[step - 1],
            send_sem=self.send_sem.at[self.axis, step],
            recv_sem=self.recv_sem.at[self.axis, step],
            device_id=device_at(there, self.sizes),
            device_id_type=MESH,
        )

    def start(self):
        for step in range(1, self.sizes[self.axis]):
            self.copy(step).start()

    def finish(self):
        for step in range(1, self.sizes[self.axis]):
            self.copy(step).wait()
        mine = self.part(self.at[self.axis])
        lead = self.sizes[: self.axis]
        total = math.prod(lead)

        def add(index, _):
            where = []
            for size in reversed(lead):
                where.insert(0, lax.rem(index, size))
                index = index // size
            where = tuple(where)
            value = mine[where].astype(jnp.float32)
            for step in range(self.sizes[self.axis] - 1):
                value = value + self.landed[(step,) + where].astype(jnp.float32)
            self.out[where] = value.astype(self.out.dtype)
            return 0

        lax.fori_loop(0, total, add, 0)


class Gather:
    def __init__(self, sizes, axis, full, first, sems):
        self.sizes, self.axis, self.full, self.first = sizes, axis, full, first
        self.send_sem, self.recv_sem = sems
        self.at = coordinates(sizes)

    def copy(self, step):
        there, _ = moved(self.at, self.sizes, self.axis, step)
        where = (slice(None),) * (self.axis - self.first) + tuple(self.at[self.axis :])
        return pltpu.make_async_remote_copy(
            src_ref=self.full.at[where],
            dst_ref=self.full.at[where],
            send_sem=self.send_sem.at[self.axis, step],
            recv_sem=self.recv_sem.at[self.axis, step],
            device_id=device_at(there, self.sizes),
            device_id_type=MESH,
        )

    def start(self):
        for step in range(1, self.sizes[self.axis]):
            self.copy(step).start()

    def finish(self):
        for step in range(1, self.sizes[self.axis]):
            self.copy(step).wait()


def stage_scratch(sizes, piece):
    out = []
    for axis in range(3, -1, -1):
        shape = tuple(sizes[:axis]) + piece
        out.append(pltpu.VMEM((sizes[axis] - 1,) + shape, jnp.bfloat16))
        if axis:
            out.append(pltpu.VMEM(shape, jnp.bfloat16))
    return out


def stage_sems(sizes):
    most = max(sizes)
    return [pltpu.SemaphoreType.DMA((4, most)) for _ in range(4)]


def scatter_stages(sizes, src, bufs, result, sems):
    stages = []
    for number, axis in enumerate(range(3, -1, -1)):
        landed = bufs[2 * number]
        out = bufs[2 * number + 1] if axis else result
        stages.append(Scatter(sizes, axis, src, landed, out, sems))
        src = out
    return stages


def smooth_kernel(sizes, depth, frames, own, rim, z_ref, r_ref, x_ref, w_ref, gram_ref,
                  out_ref, rows_ref, y_ref, full, up_ref, down_ref, below, above, picked_ref,
                  regrouped, halo_send, halo_recv, all_send, all_recv,
                  s_send, s_recv, g_send, g_recv, *bufs):
    kinds = w_ref.shape[0]
    steps = y_ref.shape[0] // (2 * kinds * depth)
    groups, slabs = sizes[0] * sizes[1], sizes[2] * sizes[3]
    slab, grp = lax.axis_index("slab"), lax.axis_index("grp")
    at = coordinates(sizes)
    runs = own // groups
    upper = lax.rem(slab + 1, slabs)
    lower = lax.rem(slab + slabs - 1, slabs)

    barrier, count = greet_all(sizes)
    for other in (upper, lower):
        pl.semaphore_signal(barrier, inc=1, device_id=(other, grp), device_id_type=MESH)
    for step in range(1, groups):
        pl.semaphore_signal(
            barrier, inc=1, device_id=(slab, lax.rem(grp + step, groups)), device_id_type=MESH
        )
    pl.semaphore_wait(barrier, count + 2 + groups - 1)

    scatter = scatter_stages(sizes, gram_ref, bufs, full.at[at[2], at[3]], (s_send, s_recv))
    gather = [Gather(sizes, axis, full, 2, (g_send, g_recv)) for axis in (2, 3)]

    def planar(step, _):
        for kind in range(kinds):
            place = step * kinds + kind
            begin = pl.multiple_of(place * WIDE, WIDE)
            found = jnp.dot(
                x_ref[:, pl.ds(begin, SPAN)], w_ref[kind], preferred_element_type=jnp.float32
            )
            for side in range(2):
                y_ref[pl.ds((2 * place + side) * depth, depth)] = found[
                    :, side * RUN : (side + 1) * RUN
                ].reshape(depth, frames, RUN)
        return 0

    def picked(run):
        total = None
        for tap in range(2 * RAD + 1):
            term = z_ref[run * (2 * RAD + 1) + tap] * y_ref[r_ref[run * (2 * RAD + 1) + tap]]
            total = term if total is None else total + term
        return total

    def put(ref, first):
        def one(run, _):
            ref[run] = picked(run + first).astype(ref.dtype)
            return 0

        lax.fori_loop(0, rim, one, 0)

    def halo(src, dst, number, other):
        return pltpu.make_async_remote_copy(
            src_ref=src, dst_ref=dst, send_sem=halo_send.at[number], recv_sem=halo_recv.at[number],
            device_id=(other, grp), device_id_type=MESH,
        )

    scatter[0].start()
    early = steps // 3
    lax.fori_loop(0, early, planar, 0)
    scatter[0].finish()
    scatter[1].start()
    lax.fori_loop(early, steps, planar, 0)

    put(up_ref, own)
    halo_up = halo(up_ref, below, 0, upper)
    halo_up.start()
    put(down_ref, own + rim)
    halo_down = halo(down_ref, above, 1, lower)
    halo_down.start()

    def inner(run, _):
        picked_ref[run] = picked(run).astype(picked_ref.dtype)
        return 0

    lax.fori_loop(rim, own - rim, inner, 0)
    halo_up.wait()
    halo_down.wait()
    low_part = jnp.where(slab > 0, 1.0, 0.0)
    high_part = jnp.where(slab < slabs - 1, 1.0, 0.0)

    def edge(run, _):
        picked_ref[run] = (picked(run) + low_part * below[run].astype(jnp.float32)).astype(
            picked_ref.dtype
        )
        last = run + own - rim
        picked_ref[last] = (picked(last) + high_part * above[run].astype(jnp.float32)).astype(
            picked_ref.dtype
        )
        return 0

    lax.fori_loop(0, rim, edge, 0)

    def trade(step):
        other = lax.rem(grp + step, groups)
        return pltpu.make_async_remote_copy(
            src_ref=picked_ref.at[pl.ds(other * runs, runs)], dst_ref=regrouped.at[grp],
            send_sem=all_send.at[step], recv_sem=all_recv.at[step],
            device_id=(slab, other), device_id_type=MESH,
        )

    for step in range(1, groups):
        trade(step).start()
    regrouped[grp] = picked_ref[pl.ds(grp * runs, runs)]

    scatter[1].finish()
    for stage in scatter[2:]:
        stage.start()
        stage.finish()
    for stage in gather:
        stage.start()
        stage.finish()
    for step in range(1, groups):
        trade(step).wait()
    rows_ref[...] = full[...]

    half = groups // 2
    for run in range(runs):
        lanes = slice(run * RUN, (run + 1) * RUN)
        for subject in range(2):
            block = regrouped[subject * half : (subject + 1) * half, run].astype(jnp.float32)
            block = block.reshape(half * frames, RUN)
            mean = jnp.sum(block, axis=0, keepdims=True) * (1.0 / (half * frames))
            out_ref[subject * half * frames : (subject + 1) * half * frames, lanes] = (
                block - mean
            ).astype(out_ref.dtype)


def smooth(cells, weights, planes_at, runs_at, gram, sizes, depth, frames, extent, own, rim):
    vmem = pl.BlockSpec(memory_space=pltpu.VMEM)
    smem = pl.BlockSpec(memory_space=pltpu.SMEM)
    groups = sizes[0] * sizes[1]
    runs = own // groups
    piece = gram.shape[4:]
    rim_shape = pltpu.VMEM((rim, frames, RUN), jnp.bfloat16)
    return pl.pallas_call(
        functools.partial(smooth_kernel, sizes, depth, frames, own, rim),
        out_shape=(
            jax.ShapeDtypeStruct((groups * frames, runs * RUN), jnp.bfloat16),
            jax.ShapeDtypeStruct(tuple(sizes[2:]) + piece, jnp.bfloat16),
        ),
        in_specs=[smem, smem, vmem, vmem, vmem],
        out_specs=(vmem, vmem),
        scratch_shapes=[
            pltpu.VMEM((extent // RUN * depth, frames, RUN), jnp.float32),
            pltpu.VMEM(tuple(sizes[2:]) + piece, jnp.bfloat16),
            rim_shape, rim_shape, rim_shape, rim_shape,
            pltpu.VMEM((own, frames, RUN), jnp.bfloat16),
            pltpu.VMEM((groups, runs, frames, RUN), jnp.bfloat16),
            pltpu.SemaphoreType.DMA((2,)),
            pltpu.SemaphoreType.DMA((2,)),
            pltpu.SemaphoreType.DMA((groups,)),
            pltpu.SemaphoreType.DMA((groups,)),
        ]
        + stage_sems(sizes)
        + stage_scratch(sizes, piece),
        compiler_params=pltpu.CompilerParams(
            collective_id=2, has_side_effects=True, vmem_limit_bytes=60 * 1024 * 1024
        ),
    )(planes_at, runs_at, cells, weights, gram)


def sum_kernel(sizes, part_ref, out_ref, full, s_send, s_recv, g_send, g_recv, *bufs):
    at = coordinates(sizes)
    barrier, count = greet_all(sizes)
    pl.semaphore_wait(barrier, count)
    for stage in scatter_stages(sizes, part_ref, bufs, full.at[tuple(at)], (s_send, s_recv)):
        stage.start()
        stage.finish()
    for axis in range(4):
        stage = Gather(sizes, axis, full, 0, (g_send, g_recv))
        stage.start()
        stage.finish()
    out_ref[...] = full[...]


def sum_over_all(part, sizes):
    piece = part.shape[4:]
    vmem = pl.BlockSpec(memory_space=pltpu.VMEM)
    return pl.pallas_call(
        functools.partial(sum_kernel, sizes),
        out_shape=jax.ShapeDtypeStruct(part.shape, part.dtype),
        in_specs=[vmem],
        out_specs=vmem,
        scratch_shapes=[pltpu.VMEM(part.shape, part.dtype)]
        + stage_sems(sizes)
        + stage_scratch(sizes, piece),
        compiler_params=pltpu.CompilerParams(collective_id=3, has_side_effects=True),
    )(part)


def body(raw_frames, mask_index, subspace, rotation):
    frames_here, slab_depth, extent = raw_frames.shape
    per_device = subspace.shape[1]
    group_count = lax.axis_size("grp")
    slab_count = lax.axis_size("slab")
    sizes = axes_of(group_count, slab_count)
    masked = per_device * slab_count * group_count
    frame_count = frames_here * group_count
    subject_frames = frame_count // 2
    order_rows = K + frame_count
    rows_here = order_rows // group_count
    first_row = lax.axis_index("grp") * rows_here
    slab = lax.axis_index("slab")
    runs_here = per_device // RUN
    own = runs_here * group_count
    rim = own * RAD // slab_depth
    across = (((1,), (1,)), ((), ()))

    starts = exchange(mask_index.reshape(runs_here, RUN), False, 1)[:, :, 0]
    starts = starts.reshape(slab_count, own) - slab * (slab_depth * extent)
    wanted = jnp.concatenate(
        [
            lax.dynamic_index_in_dim(starts, slab, 0, False),
            lax.dynamic_index_in_dim(starts, jnp.minimum(slab + 1, slab_count - 1), 0, False)[:rim],
            lax.dynamic_index_in_dim(starts, jnp.maximum(slab - 1, 0), 0, False)[own - rim :],
        ]
    )
    planes_at = jnp.floor_divide(wanted, extent)
    runs_at = (wanted - planes_at * extent) // RUN
    planes = planes_at[:, None] + jnp.arange(-RAD, RAD + 1, dtype=jnp.int32)[None, :]
    taps = jnp.asarray(tap_weights(), jnp.float32)[None, :]
    weight_at = jnp.where((planes >= 0) & (planes < slab_depth), taps, 0.0).reshape(-1)
    cell_at = runs_at[:, None] * slab_depth + jnp.clip(planes, 0, slab_depth - 1)
    cell_at = cell_at.reshape(-1)

    basis_part = lax.dot_general(
        subspace, subspace, across, preferred_element_type=jnp.float32
    ).astype(jnp.bfloat16)
    share = -(-rows_here // (16 * slab_count)) * 16
    basis_part = jnp.pad(basis_part, ((0, frame_count), (0, 0))).reshape(group_count, rows_here, K)
    basis_part = jnp.pad(basis_part, ((0, 0), (0, share * slab_count - rows_here), (0, 0)))
    basis_part = basis_part.reshape(tuple(sizes) + (share, K))

    cells = jnp.pad(
        raw_frames.transpose(1, 0, 2), ((0, 0), (0, 0), (LEFT, SPAN - WIDE - LEFT))
    ).reshape(slab_depth * frames_here, -1)
    centered, basis_rows = smooth(
        cells, jnp.asarray(plane_weights()), weight_at, cell_at, basis_part,
        sizes, slab_depth, frames_here, extent, own, rim,
    )
    basis_rows = basis_rows.reshape(share * slab_count, K)[:rows_here].astype(jnp.float32)

    stacked = jnp.concatenate([subspace, centered], 0)
    data_part = lax.dot_general(
        centered, stacked, across, preferred_element_type=jnp.float32
    ).astype(jnp.bfloat16)
    data_part = data_part.reshape(tuple(sizes) + (-1, order_rows))
    data = sum_over_all(data_part, sizes).reshape(frame_count, order_rows).astype(jnp.float32)
    power = jnp.sum(jnp.diagonal(data[:, K:]).reshape(2, subject_frames), axis=1)
    scales = lax.rsqrt(power / (masked * subject_frames) + epsilon)
    row_scale = jnp.concatenate([jnp.ones((K,), jnp.float32), jnp.repeat(scales, subject_frames)])

    turned = (rotation.astype(jnp.float32) * row_scale[:, None]).astype(jnp.bfloat16)
    new_subspace = lax.dot_general(
        turned, stacked, (((0,), (0,)), ((), ())), preferred_element_type=jnp.float32
    ).astype(jnp.bfloat16)

    right = lax.dynamic_slice_in_dim(data, first_row, rows_here, 1).T
    low = jnp.pad(data[:, :K], ((rows_here, rows_here), (0, 0)))
    low = lax.dynamic_slice_in_dim(low, jnp.maximum(first_row - K + rows_here, 0), rows_here, 0)
    owned = jnp.concatenate([basis_rows + low, right], 1)
    owned_scale = lax.dynamic_slice_in_dim(row_scale, first_row, rows_here, 0)
    gram_rows = owned * (owned_scale[:, None] * row_scale[None, :]) / masked
    return (gram_rows, new_subspace)


def solution(mesh):
    placed = (P("grp", "slab", None), P(("slab", "grp")), P(None, ("slab", "grp")), P())
    return jax.shard_map(
        body,
        mesh=mesh,
        in_specs=placed,
        out_specs=(P("grp", None), P(None, ("slab", "grp"))),
        check_vma=False,
    )
```

```python
import functools
import math

import jax
import jax.numpy as jnp
import numpy as np
from jax import lax
from jax.experimental import pallas as pl
from jax.experimental.pallas import tpu as pltpu
from jax.sharding import PartitionSpec as P

NX = 96
RUN = 128
RAD = 3
K = 1200
MESH = pl.DeviceIdType.MESH

smooth_sigma = 1.0617
epsilon = 1e-06

WIDE = 2 * RUN
LEFT = 3 * RUN
SPAN = 8 * RUN


def tap_weights():
    unscaled = [
        math.exp(-offset * offset / (2.0 * smooth_sigma * smooth_sigma))
        for offset in range(-RAD, RAD + 1)
    ]
    summed = sum(unscaled)
    return [weight / summed for weight in unscaled]


def plane_weights():
    taps = np.array(tap_weights())
    kinds = NX // math.gcd(WIDE, NX)
    out = np.zeros((kinds, SPAN, WIDE))
    for kind in range(kinds):
        target = np.arange(WIDE)
        column = (kind * WIDE + target) % NX
        for dy in range(-RAD, RAD + 1):
            for dx in range(-RAD, RAD + 1):
                inside = (column + dx >= 0) & (column + dx < NX)
                source = target + LEFT + dy * NX + dx
                out[kind, source[inside], target[inside]] = taps[dy + RAD] * taps[dx + RAD]
    return out.astype(jnp.bfloat16)


def exchange_kernel(total, groups, summed, x_ref, out_ref, landed, send_sem, recv_sem):
    me = lax.axis_index("slab") * groups + lax.axis_index("grp")
    barrier = pltpu.get_barrier_semaphore()

    def place(peer):
        return (peer // groups, lax.rem(peer, groups))

    def greet(step, _):
        pl.semaphore_signal(
            barrier, inc=1, device_id=place(lax.rem(me + step, total)), device_id_type=MESH
        )
        return 0

    lax.fori_loop(1, total, greet, 0)
    pl.semaphore_wait(barrier, total - 1)

    def copy(step):
        return pltpu.make_async_remote_copy(
            src_ref=x_ref,
            dst_ref=landed.at[step],
            send_sem=send_sem.at[step],
            recv_sem=recv_sem.at[step],
            device_id=place(lax.rem(me + step, total)),
            device_id_type=MESH,
        )

    def start(step, _):
        copy(step).start()
        return 0

    def finish(step, _):
        copy(step).wait()
        return 0

    lax.fori_loop(1, total, start, 0)
    landed[0] = x_ref[...]
    lax.fori_loop(1, total, finish, 0)
    if summed:
        out_ref[...] = jnp.sum(landed[...], axis=0)
    else:
        def put(step, _):
            out_ref[lax.rem(me + total - step, total)] = landed[step]
            return 0

        lax.fori_loop(0, total, put, 0)


def exchange(x, summed, collective_id):
    groups = lax.axis_size("grp")
    total = groups * lax.axis_size("slab")
    shape = x.shape if summed else (total,) + x.shape
    return pl.pallas_call(
        functools.partial(exchange_kernel, total, groups, summed),
        out_shape=jax.ShapeDtypeStruct(shape, x.dtype),
        in_specs=[pl.BlockSpec(memory_space=pltpu.VMEM)],
        out_specs=pl.BlockSpec(memory_space=pltpu.VMEM),
        scratch_shapes=[
            pltpu.VMEM((total,) + x.shape, x.dtype),
            pltpu.SemaphoreType.DMA((total,)),
            pltpu.SemaphoreType.DMA((total,)),
        ],
        compiler_params=pltpu.CompilerParams(
            collective_id=collective_id, has_side_effects=True
        ),
    )(x)


def axes_of(groups, slabs):
    outer = 4 if groups % 4 == 0 else 1
    cores = 2 if slabs % 2 == 0 else 1
    return outer, groups // outer, slabs // cores, cores


def coordinates(sizes):
    slab, grp = lax.axis_index("slab"), lax.axis_index("grp")
    return [grp // sizes[1], lax.rem(grp, sizes[1]), slab // sizes[3], lax.rem(slab, sizes[3])]


def device_at(at, sizes):
    return (at[2] * sizes[3] + at[3], at[0] * sizes[1] + at[1])


def moved(at, sizes, axis, step):
    other = lax.rem(at[axis] + step, sizes[axis])
    return at[:axis] + [other] + at[axis + 1 :], other


def greet_all(sizes):
    barrier = pltpu.get_barrier_semaphore()
    at = coordinates(sizes)
    count = 0
    for axis, size in enumerate(sizes):
        for step in range(1, size):
            there, _ = moved(at, sizes, axis, step)
            pl.semaphore_signal(
                barrier, inc=1, device_id=device_at(there, sizes), device_id_type=MESH
            )
            count += 1
    return barrier, count


class Scatter:
    def __init__(self, sizes, axis, left, src, landed, out, sems):
        self.sizes, self.axis, self.src, self.landed, self.out = sizes, axis, src, landed, out
        self.dim = left.index(axis)
        self.left = [other for other in left if other != axis]
        self.send_sem, self.recv_sem = sems
        self.at = coordinates(sizes)

    def part(self, where):
        return self.src.at[(slice(None),) * self.dim + (where,)]

    def copy(self, step):
        there, other = moved(self.at, self.sizes, self.axis, step)
        return pltpu.make_async_remote_copy(
            src_ref=self.part(other),
            dst_ref=self.landed.at[step - 1],
            send_sem=self.send_sem.at[self.axis, step],
            recv_sem=self.recv_sem.at[self.axis, step],
            device_id=device_at(there, self.sizes),
            device_id_type=MESH,
        )

    def start(self):
        for step in range(1, self.sizes[self.axis]):
            self.copy(step).start()

    def finish(self):
        for step in range(1, self.sizes[self.axis]):
            self.copy(step).wait()
        mine = self.part(self.at[self.axis])
        lead = [self.sizes[axis] for axis in self.left]
        total = math.prod(lead)

        def add(index, _):
            where = []
            for size in reversed(lead):
                where.insert(0, lax.rem(index, size))
                index = index // size
            where = tuple(where)
            value = mine[where].astype(jnp.float32)
            for step in range(self.sizes[self.axis] - 1):
                value = value + self.landed[(step,) + where].astype(jnp.float32)
            self.out[where] = value.astype(self.out.dtype)
            return 0

        lax.fori_loop(0, total, add, 0)


class Gather:
    def __init__(self, sizes, axis, full, first, sems):
        self.sizes, self.axis, self.full, self.first = sizes, axis, full, first
        self.send_sem, self.recv_sem = sems
        self.at = coordinates(sizes)

    def copy(self, step):
        there, _ = moved(self.at, self.sizes, self.axis, step)
        where = (slice(None),) * (self.axis - self.first) + tuple(self.at[self.axis :])
        return pltpu.make_async_remote_copy(
            src_ref=self.full.at[where],
            dst_ref=self.full.at[where],
            send_sem=self.send_sem.at[self.axis, step],
            recv_sem=self.recv_sem.at[self.axis, step],
            device_id=device_at(there, self.sizes),
            device_id_type=MESH,
        )

    def start(self):
        for step in range(1, self.sizes[self.axis]):
            self.copy(step).start()

    def finish(self):
        for step in range(1, self.sizes[self.axis]):
            self.copy(step).wait()


STAGES = (3, 1, 2, 0)


def stage_scratch(sizes, piece):
    out = []
    left = [0, 1, 2, 3]
    for axis in STAGES:
        left.remove(axis)
        shape = tuple(sizes[other] for other in left) + piece
        out.append(pltpu.VMEM((sizes[axis] - 1,) + shape, jnp.bfloat16))
        if left:
            out.append(pltpu.VMEM(shape, jnp.bfloat16))
    return out


def stage_sems(sizes):
    most = max(sizes)
    return [pltpu.SemaphoreType.DMA((4, most)) for _ in range(4)]


def scatter_stages(sizes, src, bufs, result, sems):
    stages = []
    left = [0, 1, 2, 3]
    for number, axis in enumerate(STAGES):
        last = number == len(STAGES) - 1
        out = result if last else bufs[2 * number + 1]
        stages.append(Scatter(sizes, axis, left, src, bufs[2 * number], out, sems))
        left = stages[-1].left
        src = out
    return stages


def smooth_kernel(sizes, depth, frames, own, rim, z_ref, r_ref, x_ref, w_ref, gram_ref,
                  out_ref, rows_ref, y_ref, full, up_ref, down_ref, below, above, picked_ref,
                  regrouped, halo_send, halo_recv, all_send, all_recv,
                  s_send, s_recv, g_send, g_recv, *bufs):
    kinds = w_ref.shape[0]
    steps = y_ref.shape[0] // (2 * kinds * depth)
    groups, slabs = sizes[0] * sizes[1], sizes[2] * sizes[3]
    slab, grp = lax.axis_index("slab"), lax.axis_index("grp")
    at = coordinates(sizes)
    runs = own // groups
    upper = lax.rem(slab + 1, slabs)
    lower = lax.rem(slab + slabs - 1, slabs)

    barrier, count = greet_all(sizes)
    for other in (upper, lower):
        pl.semaphore_signal(barrier, inc=1, device_id=(other, grp), device_id_type=MESH)
    for step in range(1, groups):
        pl.semaphore_signal(
            barrier, inc=1, device_id=(slab, lax.rem(grp + step, groups)), device_id_type=MESH
        )
    pl.semaphore_wait(barrier, count + 2 + groups - 1)

    scatter = scatter_stages(sizes, gram_ref, bufs, full.at[at[2], at[3]], (s_send, s_recv))
    gather = [Gather(sizes, axis, full, 2, (g_send, g_recv)) for axis in (2, 3)]

    def planar(step, _):
        for kind in range(kinds):
            place = step * kinds + kind
            begin = pl.multiple_of(place * WIDE, WIDE)
            found = jnp.dot(
                x_ref[:, pl.ds(begin, SPAN)], w_ref[kind], preferred_element_type=jnp.float32
            )
            for side in range(2):
                y_ref[pl.ds((2 * place + side) * depth, depth)] = found[
                    :, side * RUN : (side + 1) * RUN
                ].reshape(depth, frames, RUN)
        return 0

    def picked(run):
        total = None
        for tap in range(2 * RAD + 1):
            term = z_ref[run * (2 * RAD + 1) + tap] * y_ref[r_ref[run * (2 * RAD + 1) + tap]]
            total = term if total is None else total + term
        return total

    def put(ref, first):
        def one(run, _):
            ref[run] = picked(run + first).astype(ref.dtype)
            return 0

        lax.fori_loop(0, rim, one, 0)

    def halo(src, dst, number, other):
        return pltpu.make_async_remote_copy(
            src_ref=src, dst_ref=dst, send_sem=halo_send.at[number], recv_sem=halo_recv.at[number],
            device_id=(other, grp), device_id_type=MESH,
        )

    scatter[0].start()
    early = steps // 3
    lax.fori_loop(0, early, planar, 0)
    scatter[0].finish()
    scatter[1].start()
    lax.fori_loop(early, steps, planar, 0)

    put(up_ref, own)
    halo_up = halo(up_ref, below, 0, upper)
    halo_up.start()
    put(down_ref, own + rim)
    halo_down = halo(down_ref, above, 1, lower)
    halo_down.start()

    def inner(run, _):
        picked_ref[run] = picked(run).astype(picked_ref.dtype)
        return 0

    lax.fori_loop(rim, own - rim, inner, 0)
    halo_up.wait()
    halo_down.wait()
    low_part = jnp.where(slab > 0, 1.0, 0.0)
    high_part = jnp.where(slab < slabs - 1, 1.0, 0.0)

    def edge(run, _):
        picked_ref[run] = (picked(run) + low_part * below[run].astype(jnp.float32)).astype(
            picked_ref.dtype
        )
        last = run + own - rim
        picked_ref[last] = (picked(last) + high_part * above[run].astype(jnp.float32)).astype(
            picked_ref.dtype
        )
        return 0

    lax.fori_loop(0, rim, edge, 0)

    def trade(step):
        other = lax.rem(grp + step, groups)
        return pltpu.make_async_remote_copy(
            src_ref=picked_ref.at[pl.ds(other * runs, runs)], dst_ref=regrouped.at[grp],
            send_sem=all_send.at[step], recv_sem=all_recv.at[step],
            device_id=(slab, other), device_id_type=MESH,
        )

    for step in range(1, groups):
        trade(step).start()
    regrouped[grp] = picked_ref[pl.ds(grp * runs, runs)]

    scatter[1].finish()
    for stage in scatter[2:]:
        stage.start()
        stage.finish()
    for stage in gather:
        stage.start()
        stage.finish()
    for step in range(1, groups):
        trade(step).wait()
    rows_ref[...] = full[...]

    half = groups // 2
    for run in range(runs):
        lanes = slice(run * RUN, (run + 1) * RUN)
        for subject in range(2):
            block = regrouped[subject * half : (subject + 1) * half, run].astype(jnp.float32)
            block = block.reshape(half * frames, RUN)
            mean = jnp.sum(block, axis=0, keepdims=True) * (1.0 / (half * frames))
            out_ref[subject * half * frames : (subject + 1) * half * frames, lanes] = (
                block - mean
            ).astype(out_ref.dtype)


def smooth(cells, weights, planes_at, runs_at, gram, sizes, depth, frames, extent, own, rim):
    vmem = pl.BlockSpec(memory_space=pltpu.VMEM)
    smem = pl.BlockSpec(memory_space=pltpu.SMEM)
    groups = sizes[0] * sizes[1]
    runs = own // groups
    piece = gram.shape[4:]
    rim_shape = pltpu.VMEM((rim, frames, RUN), jnp.bfloat16)
    return pl.pallas_call(
        functools.partial(smooth_kernel, sizes, depth, frames, own, rim),
        out_shape=(
            jax.ShapeDtypeStruct((groups * frames, runs * RUN), jnp.bfloat16),
            jax.ShapeDtypeStruct(tuple(sizes[2:]) + piece, jnp.bfloat16),
        ),
        in_specs=[smem, smem, vmem, vmem, vmem],
        out_specs=(vmem, vmem),
        scratch_shapes=[
            pltpu.VMEM((extent // RUN * depth, frames, RUN), jnp.float32),
            pltpu.VMEM(tuple(sizes[2:]) + piece, jnp.bfloat16),
            rim_shape, rim_shape, rim_shape, rim_shape,
            pltpu.VMEM((own, frames, RUN), jnp.bfloat16),
            pltpu.VMEM((groups, runs, frames, RUN), jnp.bfloat16),
            pltpu.SemaphoreType.DMA((2,)),
            pltpu.SemaphoreType.DMA((2,)),
            pltpu.SemaphoreType.DMA((groups,)),
            pltpu.SemaphoreType.DMA((groups,)),
        ]
        + stage_sems(sizes)
        + stage_scratch(sizes, piece),
        compiler_params=pltpu.CompilerParams(
            collective_id=2, has_side_effects=True, vmem_limit_bytes=60 * 1024 * 1024
        ),
    )(planes_at, runs_at, cells, weights, gram)


def sum_kernel(sizes, part_ref, out_ref, full, s_send, s_recv, g_send, g_recv, *bufs):
    at = coordinates(sizes)
    barrier, count = greet_all(sizes)
    pl.semaphore_wait(barrier, count)
    for stage in scatter_stages(sizes, part_ref, bufs, full.at[tuple(at)], (s_send, s_recv)):
        stage.start()
        stage.finish()
    for axis in range(4):
        stage = Gather(sizes, axis, full, 0, (g_send, g_recv))
        stage.start()
        stage.finish()
    out_ref[...] = full[...]


def sum_over_all(part, sizes):
    piece = part.shape[4:]
    vmem = pl.BlockSpec(memory_space=pltpu.VMEM)
    return pl.pallas_call(
        functools.partial(sum_kernel, sizes),
        out_shape=jax.ShapeDtypeStruct(part.shape, part.dtype),
        in_specs=[vmem],
        out_specs=vmem,
        scratch_shapes=[pltpu.VMEM(part.shape, part.dtype)]
        + stage_sems(sizes)
        + stage_scratch(sizes, piece),
        compiler_params=pltpu.CompilerParams(collective_id=3, has_side_effects=True),
    )(part)


def body(raw_frames, mask_index, subspace, rotation):
    frames_here, slab_depth, extent = raw_frames.shape
    per_device = subspace.shape[1]
    group_count = lax.axis_size("grp")
    slab_count = lax.axis_size("slab")
    sizes = axes_of(group_count, slab_count)
    masked = per_device * slab_count * group_count
    frame_count = frames_here * group_count
    subject_frames = frame_count // 2
    order_rows = K + frame_count
    rows_here = order_rows // group_count
    first_row = lax.axis_index("grp") * rows_here
    slab = lax.axis_index("slab")
    runs_here = per_device // RUN
    own = runs_here * group_count
    rim = own * RAD // slab_depth
    across = (((1,), (1,)), ((), ()))

    starts = jnp.pad(mask_index.reshape(runs_here, RUN)[:, 0], (0, RUN - runs_here))
    starts = exchange(starts.reshape(1, RUN), False, 1)[:, 0, :runs_here]
    starts = starts.reshape(slab_count, own) - slab * (slab_depth * extent)
    wanted = jnp.concatenate(
        [
            lax.dynamic_index_in_dim(starts, slab, 0, False),
            lax.dynamic_index_in_dim(starts, jnp.minimum(slab + 1, slab_count - 1), 0, False)[:rim],
            lax.dynamic_index_in_dim(starts, jnp.maximum(slab - 1, 0), 0, False)[own - rim :],
        ]
    )
    planes_at = jnp.floor_divide(wanted, extent)
    runs_at = (wanted - planes_at * extent) // RUN
    planes = planes_at[:, None] + jnp.arange(-RAD, RAD + 1, dtype=jnp.int32)[None, :]
    taps = jnp.asarray(tap_weights(), jnp.float32)[None, :]
    weight_at = jnp.where((planes >= 0) & (planes < slab_depth), taps, 0.0).reshape(-1)
    cell_at = runs_at[:, None] * slab_depth + jnp.clip(planes, 0, slab_depth - 1)
    cell_at = cell_at.reshape(-1)

    share = -(-rows_here // (16 * slab_count)) * 16
    spread = []
    for group in range(group_count):
        begin, end = (min(K, (group + more) * rows_here) for more in (0, 1))
        spread.append(
            jnp.pad(subspace[begin:end], ((0, share * slab_count - (end - begin)), (0, 0)))
        )
    basis_part = lax.dot_general(
        jnp.concatenate(spread), subspace, across, preferred_element_type=jnp.float32
    ).astype(jnp.bfloat16)
    basis_part = basis_part.reshape(tuple(sizes) + (share, K))

    cells = jnp.pad(
        raw_frames.transpose(1, 0, 2), ((0, 0), (0, 0), (LEFT, SPAN - WIDE - LEFT))
    ).reshape(slab_depth * frames_here, -1)
    centered, basis_rows = smooth(
        cells, jnp.asarray(plane_weights()), weight_at, cell_at, basis_part,
        sizes, slab_depth, frames_here, extent, own, rim,
    )
    basis_rows = basis_rows.reshape(share * slab_count, K)[:rows_here].astype(jnp.float32)

    stacked = jnp.concatenate([subspace, centered], 0)
    data_part = lax.dot_general(
        centered, stacked, across, preferred_element_type=jnp.float32
    ).astype(jnp.bfloat16)
    data_part = data_part.reshape(tuple(sizes) + (-1, order_rows))
    data = sum_over_all(data_part, sizes).reshape(frame_count, order_rows).astype(jnp.float32)
    power = jnp.sum(jnp.diagonal(data[:, K:]).reshape(2, subject_frames), axis=1)
    scales = lax.rsqrt(power / (masked * subject_frames) + epsilon)
    row_scale = jnp.concatenate([jnp.ones((K,), jnp.float32), jnp.repeat(scales, subject_frames)])

    turned = (rotation.astype(jnp.float32) * row_scale[:, None]).astype(jnp.bfloat16)
    new_subspace = lax.dot_general(
        turned, stacked, (((0,), (0,)), ((), ())), preferred_element_type=jnp.float32
    ).astype(jnp.bfloat16)

    right = lax.dynamic_slice_in_dim(data, first_row, rows_here, 1).T
    low = jnp.pad(data[:, :K], ((rows_here, rows_here), (0, 0)))
    low = lax.dynamic_slice_in_dim(low, jnp.maximum(first_row - K + rows_here, 0), rows_here, 0)
    owned = jnp.concatenate([basis_rows + low, right], 1)
    owned_scale = lax.dynamic_slice_in_dim(row_scale, first_row, rows_here, 0)
    gram_rows = owned * (owned_scale[:, None] * row_scale[None, :]) / masked
    return (gram_rows, new_subspace)


def solution(mesh):
    placed = (P("grp", "slab", None), P(("slab", "grp")), P(None, ("slab", "grp")), P())
    return jax.shard_map(
        body,
        mesh=mesh,
        in_specs=placed,
        out_specs=(P("grp", None), P(None, ("slab", "grp"))),
        check_vma=False,
    )
```

```python
import functools
import math

import jax
import jax.numpy as jnp
import numpy as np
from jax import lax
from jax.experimental import pallas as pl
from jax.experimental.pallas import tpu as pltpu
from jax.sharding import PartitionSpec as P

NX = 96
RUN = 128
RAD = 3
K = 1200
MESH = pl.DeviceIdType.MESH

smooth_sigma = 1.0617
epsilon = 1e-06

WIDE = 2 * RUN
LEFT = 3 * RUN
SPAN = 8 * RUN


def tap_weights():
    unscaled = [
        math.exp(-offset * offset / (2.0 * smooth_sigma * smooth_sigma))
        for offset in range(-RAD, RAD + 1)
    ]
    summed = sum(unscaled)
    return [weight / summed for weight in unscaled]


def plane_weights():
    taps = np.array(tap_weights())
    kinds = NX // math.gcd(WIDE, NX)
    out = np.zeros((kinds, SPAN, WIDE))
    for kind in range(kinds):
        target = np.arange(WIDE)
        column = (kind * WIDE + target) % NX
        for dy in range(-RAD, RAD + 1):
            for dx in range(-RAD, RAD + 1):
                inside = (column + dx >= 0) & (column + dx < NX)
                source = target + LEFT + dy * NX + dx
                out[kind, source[inside], target[inside]] = taps[dy + RAD] * taps[dx + RAD]
    return out.astype(jnp.bfloat16)


def exchange_kernel(total, groups, summed, x_ref, out_ref, landed, send_sem, recv_sem):
    me = lax.axis_index("slab") * groups + lax.axis_index("grp")
    barrier = pltpu.get_barrier_semaphore()

    def place(peer):
        return (peer // groups, lax.rem(peer, groups))

    def greet(step, _):
        pl.semaphore_signal(
            barrier, inc=1, device_id=place(lax.rem(me + step, total)), device_id_type=MESH
        )
        return 0

    lax.fori_loop(1, total, greet, 0)
    pl.semaphore_wait(barrier, total - 1)

    def copy(step):
        return pltpu.make_async_remote_copy(
            src_ref=x_ref,
            dst_ref=landed.at[step],
            send_sem=send_sem.at[step],
            recv_sem=recv_sem.at[step],
            device_id=place(lax.rem(me + step, total)),
            device_id_type=MESH,
        )

    def start(step, _):
        copy(step).start()
        return 0

    def finish(step, _):
        copy(step).wait()
        return 0

    lax.fori_loop(1, total, start, 0)
    landed[0] = x_ref[...]
    lax.fori_loop(1, total, finish, 0)
    if summed:
        out_ref[...] = jnp.sum(landed[...], axis=0)
    else:
        def put(step, _):
            out_ref[lax.rem(me + total - step, total)] = landed[step]
            return 0

        lax.fori_loop(0, total, put, 0)


def exchange(x, summed, collective_id):
    groups = lax.axis_size("grp")
    total = groups * lax.axis_size("slab")
    shape = x.shape if summed else (total,) + x.shape
    return pl.pallas_call(
        functools.partial(exchange_kernel, total, groups, summed),
        out_shape=jax.ShapeDtypeStruct(shape, x.dtype),
        in_specs=[pl.BlockSpec(memory_space=pltpu.VMEM)],
        out_specs=pl.BlockSpec(memory_space=pltpu.VMEM),
        scratch_shapes=[
            pltpu.VMEM((total,) + x.shape, x.dtype),
            pltpu.SemaphoreType.DMA((total,)),
            pltpu.SemaphoreType.DMA((total,)),
        ],
        compiler_params=pltpu.CompilerParams(
            collective_id=collective_id, has_side_effects=True
        ),
    )(x)


def axes_of(groups, slabs):
    outer = 4 if groups % 4 == 0 else 1
    cores = 2 if slabs % 2 == 0 else 1
    return outer, groups // outer, slabs // cores, cores


def coordinates(sizes):
    slab, grp = lax.axis_index("slab"), lax.axis_index("grp")
    return [grp // sizes[1], lax.rem(grp, sizes[1]), slab // sizes[3], lax.rem(slab, sizes[3])]


def device_at(at, sizes):
    return (at[2] * sizes[3] + at[3], at[0] * sizes[1] + at[1])


def moved(at, sizes, axis, step):
    other = lax.rem(at[axis] + step, sizes[axis])
    return at[:axis] + [other] + at[axis + 1 :], other


def greet_all(sizes):
    barrier = pltpu.get_barrier_semaphore()
    at = coordinates(sizes)
    count = 0
    for axis, size in enumerate(sizes):
        for step in range(1, size):
            there, _ = moved(at, sizes, axis, step)
            pl.semaphore_signal(
                barrier, inc=1, device_id=device_at(there, sizes), device_id_type=MESH
            )
            count += 1
    return barrier, count


class Scatter:
    def __init__(self, sizes, axis, left, src, landed, out, sems):
        self.sizes, self.axis, self.src, self.landed, self.out = sizes, axis, src, landed, out
        self.dim = left.index(axis)
        self.left = [other for other in left if other != axis]
        self.send_sem, self.recv_sem = sems
        self.at = coordinates(sizes)

    def part(self, where):
        return self.src.at[(slice(None),) * self.dim + (where,)]

    def copy(self, step):
        there, other = moved(self.at, self.sizes, self.axis, step)
        return pltpu.make_async_remote_copy(
            src_ref=self.part(other),
            dst_ref=self.landed.at[step - 1],
            send_sem=self.send_sem.at[self.axis, step],
            recv_sem=self.recv_sem.at[self.axis, step],
            device_id=device_at(there, self.sizes),
            device_id_type=MESH,
        )

    def start(self):
        for step in range(1, self.sizes[self.axis]):
            self.copy(step).start()

    def finish(self):
        for step in range(1, self.sizes[self.axis]):
            self.copy(step).wait()
        mine = self.part(self.at[self.axis])
        lead = [self.sizes[axis] for axis in self.left]
        total = math.prod(lead)

        def add(index, _):
            where = []
            for size in reversed(lead):
                where.insert(0, lax.rem(index, size))
                index = index // size
            where = tuple(where)
            value = mine[where].astype(jnp.float32)
            for step in range(self.sizes[self.axis] - 1):
                value = value + self.landed[(step,) + where].astype(jnp.float32)
            self.out[where] = value.astype(self.out.dtype)
            return 0

        lax.fori_loop(0, total, add, 0)


class Gather:
    def __init__(self, sizes, axis, full, first, sems):
        self.sizes, self.axis, self.full, self.first = sizes, axis, full, first
        self.send_sem, self.recv_sem = sems
        self.at = coordinates(sizes)

    def copy(self, step):
        there, _ = moved(self.at, self.sizes, self.axis, step)
        where = (slice(None),) * (self.axis - self.first) + tuple(self.at[self.axis :])
        return pltpu.make_async_remote_copy(
            src_ref=self.full.at[where],
            dst_ref=self.full.at[where],
            send_sem=self.send_sem.at[self.axis, step],
            recv_sem=self.recv_sem.at[self.axis, step],
            device_id=device_at(there, self.sizes),
            device_id_type=MESH,
        )

    def start(self):
        for step in range(1, self.sizes[self.axis]):
            self.copy(step).start()

    def finish(self):
        for step in range(1, self.sizes[self.axis]):
            self.copy(step).wait()


STAGES = (3, 1, 2, 0)


def stage_scratch(sizes, piece):
    out = []
    left = [axis for axis in range(4) if sizes[axis] > 1]
    for axis in STAGES:
        if sizes[axis] == 1:
            continue
        left.remove(axis)
        shape = tuple(sizes[other] for other in left) + piece
        out.append(pltpu.VMEM((sizes[axis] - 1,) + shape, jnp.bfloat16))
        if left:
            out.append(pltpu.VMEM(shape, jnp.bfloat16))
    return out


def stage_sems(sizes):
    most = max(sizes)
    return [pltpu.SemaphoreType.DMA((4, most)) for _ in range(4)]


def scatter_stages(sizes, src, bufs, result, sems):
    stages = []
    left = [0, 1, 2, 3]
    for axis in STAGES:
        if sizes[axis] == 1:
            src = src.at[(slice(None),) * left.index(axis) + (0,)]
            left = [other for other in left if other != axis]
    order = [axis for axis in STAGES if sizes[axis] > 1]
    for number, axis in enumerate(order):
        last = number == len(order) - 1
        out = result if last else bufs[2 * number + 1]
        stages.append(Scatter(sizes, axis, left, src, bufs[2 * number], out, sems))
        left = stages[-1].left
        src = out
    return stages


def smooth_kernel(sizes, depth, frames, own, rim, z_ref, r_ref, x_ref, w_ref, gram_ref,
                  out_ref, rows_ref, y_ref, full, up_ref, down_ref, below, above, picked_ref,
                  regrouped, halo_send, halo_recv, all_send, all_recv,
                  s_send, s_recv, g_send, g_recv, *bufs):
    kinds = w_ref.shape[0]
    steps = y_ref.shape[0] // (2 * kinds * depth)
    groups, slabs = sizes[0] * sizes[1], sizes[2] * sizes[3]
    slab, grp = lax.axis_index("slab"), lax.axis_index("grp")
    at = coordinates(sizes)
    runs = own // groups
    upper = lax.rem(slab + 1, slabs)
    lower = lax.rem(slab + slabs - 1, slabs)

    barrier, count = greet_all(sizes)
    for other in (upper, lower):
        pl.semaphore_signal(barrier, inc=1, device_id=(other, grp), device_id_type=MESH)
    for step in range(1, groups):
        pl.semaphore_signal(
            barrier, inc=1, device_id=(slab, lax.rem(grp + step, groups)), device_id_type=MESH
        )
    pl.semaphore_wait(barrier, count + 2 + groups - 1)

    scatter = scatter_stages(sizes, gram_ref, bufs, full.at[at[2], at[3]], (s_send, s_recv))
    gather = [Gather(sizes, axis, full, 2, (g_send, g_recv)) for axis in (2, 3)]

    def planar(step, _):
        for kind in range(kinds):
            place = step * kinds + kind
            begin = pl.multiple_of(place * WIDE, WIDE)
            found = jnp.dot(
                x_ref[:, pl.ds(begin, SPAN)], w_ref[kind], preferred_element_type=jnp.float32
            )
            for side in range(2):
                y_ref[pl.ds((2 * place + side) * depth, depth)] = found[
                    :, side * RUN : (side + 1) * RUN
                ].reshape(depth, frames, RUN)
        return 0

    def picked(run):
        total = None
        for tap in range(2 * RAD + 1):
            term = z_ref[run * (2 * RAD + 1) + tap] * y_ref[r_ref[run * (2 * RAD + 1) + tap]]
            total = term if total is None else total + term
        return total

    def put(ref, first):
        def one(run, _):
            ref[run] = picked(run + first).astype(ref.dtype)
            return 0

        lax.fori_loop(0, rim, one, 0)

    def halo(src, dst, number, other):
        return pltpu.make_async_remote_copy(
            src_ref=src, dst_ref=dst, send_sem=halo_send.at[number], recv_sem=halo_recv.at[number],
            device_id=(other, grp), device_id_type=MESH,
        )

    scatter[0].start()
    early = steps // 3
    lax.fori_loop(0, early, planar, 0)
    scatter[0].finish()
    scatter[1].start()
    lax.fori_loop(early, steps, planar, 0)

    put(up_ref, own)
    halo_up = halo(up_ref, below, 0, upper)
    halo_up.start()
    put(down_ref, own + rim)
    halo_down = halo(down_ref, above, 1, lower)
    halo_down.start()

    def inner(run, _):
        picked_ref[run] = picked(run).astype(picked_ref.dtype)
        return 0

    lax.fori_loop(rim, own - rim, inner, 0)

    def trade(step):
        other = lax.rem(grp + step, groups)
        return pltpu.make_async_remote_copy(
            src_ref=picked_ref.at[pl.ds(other * runs, runs)], dst_ref=regrouped.at[grp],
            send_sem=all_send.at[step], recv_sem=all_recv.at[step],
            device_id=(slab, other), device_id_type=MESH,
        )

    outer = -(-rim // runs)

    def start_trades(at_rim):
        for step in range(1, groups):
            other = lax.rem(grp + step, groups)
            inside = (other >= outer) & (other < groups - outer)
            pl.when(jnp.logical_not(inside) if at_rim else inside)(trade(step).start)

    start_trades(False)
    halo_up.wait()
    halo_down.wait()
    low_part = jnp.where(slab > 0, 1.0, 0.0)
    high_part = jnp.where(slab < slabs - 1, 1.0, 0.0)

    def edge(run, _):
        picked_ref[run] = (picked(run) + low_part * below[run].astype(jnp.float32)).astype(
            picked_ref.dtype
        )
        last = run + own - rim
        picked_ref[last] = (picked(last) + high_part * above[run].astype(jnp.float32)).astype(
            picked_ref.dtype
        )
        return 0

    lax.fori_loop(0, rim, edge, 0)

    start_trades(True)
    regrouped[grp] = picked_ref[pl.ds(grp * runs, runs)]

    scatter[1].finish()
    for stage in scatter[2:]:
        stage.start()
        stage.finish()
    for stage in gather:
        stage.start()
        stage.finish()
    for step in range(1, groups):
        trade(step).wait()
    rows_ref[...] = full[...]

    half = groups // 2
    for run in range(runs):
        lanes = slice(run * RUN, (run + 1) * RUN)
        for subject in range(2):
            block = regrouped[subject * half : (subject + 1) * half, run].astype(jnp.float32)
            block = block.reshape(half * frames, RUN)
            mean = jnp.sum(block, axis=0, keepdims=True) * (1.0 / (half * frames))
            out_ref[subject * half * frames : (subject + 1) * half * frames, lanes] = (
                block - mean
            ).astype(out_ref.dtype)


def smooth(cells, weights, planes_at, runs_at, gram, sizes, depth, frames, extent, own, rim):
    vmem = pl.BlockSpec(memory_space=pltpu.VMEM)
    smem = pl.BlockSpec(memory_space=pltpu.SMEM)
    groups = sizes[0] * sizes[1]
    runs = own // groups
    piece = gram.shape[4:]
    rim_shape = pltpu.VMEM((rim, frames, RUN), jnp.bfloat16)
    return pl.pallas_call(
        functools.partial(smooth_kernel, sizes, depth, frames, own, rim),
        out_shape=(
            jax.ShapeDtypeStruct((groups * frames, runs * RUN), jnp.bfloat16),
            jax.ShapeDtypeStruct(tuple(sizes[2:]) + piece, jnp.bfloat16),
        ),
        in_specs=[smem, smem, vmem, vmem, vmem],
        out_specs=(vmem, vmem),
        scratch_shapes=[
            pltpu.VMEM((extent // RUN * depth, frames, RUN), jnp.float32),
            pltpu.VMEM(tuple(sizes[2:]) + piece, jnp.bfloat16),
            rim_shape, rim_shape, rim_shape, rim_shape,
            pltpu.VMEM((own, frames, RUN), jnp.bfloat16),
            pltpu.VMEM((groups, runs, frames, RUN), jnp.bfloat16),
            pltpu.SemaphoreType.DMA((2,)),
            pltpu.SemaphoreType.DMA((2,)),
            pltpu.SemaphoreType.DMA((groups,)),
            pltpu.SemaphoreType.DMA((groups,)),
        ]
        + stage_sems(sizes)
        + stage_scratch(sizes, piece),
        compiler_params=pltpu.CompilerParams(
            collective_id=2, has_side_effects=True, vmem_limit_bytes=60 * 1024 * 1024
        ),
    )(planes_at, runs_at, cells, weights, gram)


def sum_kernel(sizes, part_ref, out_ref, full, s_send, s_recv, g_send, g_recv, *bufs):
    at = coordinates(sizes)
    barrier, count = greet_all(sizes)
    pl.semaphore_wait(barrier, count)
    for stage in scatter_stages(sizes, part_ref, bufs, full.at[tuple(at)], (s_send, s_recv)):
        stage.start()
        stage.finish()
    for axis in range(4):
        stage = Gather(sizes, axis, full, 0, (g_send, g_recv))
        stage.start()
        stage.finish()
    out_ref[...] = full[...]


def sum_over_all(part, sizes):
    piece = part.shape[4:]
    vmem = pl.BlockSpec(memory_space=pltpu.VMEM)
    return pl.pallas_call(
        functools.partial(sum_kernel, sizes),
        out_shape=jax.ShapeDtypeStruct(part.shape, part.dtype),
        in_specs=[vmem],
        out_specs=vmem,
        scratch_shapes=[pltpu.VMEM(part.shape, part.dtype)]
        + stage_sems(sizes)
        + stage_scratch(sizes, piece),
        compiler_params=pltpu.CompilerParams(collective_id=3, has_side_effects=True),
    )(part)


def body(raw_frames, mask_index, subspace, rotation):
    frames_here, slab_depth, extent = raw_frames.shape
    per_device = subspace.shape[1]
    group_count = lax.axis_size("grp")
    slab_count = lax.axis_size("slab")
    sizes = axes_of(group_count, slab_count)
    masked = per_device * slab_count * group_count
    frame_count = frames_here * group_count
    subject_frames = frame_count // 2
    order_rows = K + frame_count
    rows_here = order_rows // group_count
    first_row = lax.axis_index("grp") * rows_here
    slab = lax.axis_index("slab")
    runs_here = per_device // RUN
    own = runs_here * group_count
    rim = own * RAD // slab_depth
    across = (((1,), (1,)), ((), ()))

    starts = jnp.pad(mask_index.reshape(runs_here, RUN)[:, 0], (0, RUN - runs_here))
    starts = exchange(starts.reshape(1, RUN), False, 1)[:, 0, :runs_here]
    starts = starts.reshape(slab_count, own) - slab * (slab_depth * extent)
    wanted = jnp.concatenate(
        [
            lax.dynamic_index_in_dim(starts, slab, 0, False),
            lax.dynamic_index_in_dim(starts, jnp.minimum(slab + 1, slab_count - 1), 0, False)[:rim],
            lax.dynamic_index_in_dim(starts, jnp.maximum(slab - 1, 0), 0, False)[own - rim :],
        ]
    )
    planes_at = jnp.floor_divide(wanted, extent)
    runs_at = (wanted - planes_at * extent) // RUN
    planes = planes_at[:, None] + jnp.arange(-RAD, RAD + 1, dtype=jnp.int32)[None, :]
    taps = jnp.asarray(tap_weights(), jnp.float32)[None, :]
    weight_at = jnp.where((planes >= 0) & (planes < slab_depth), taps, 0.0).reshape(-1)
    cell_at = runs_at[:, None] * slab_depth + jnp.clip(planes, 0, slab_depth - 1)
    cell_at = cell_at.reshape(-1)

    share = -(-rows_here // (16 * slab_count)) * 16
    spread = []
    for group in range(group_count):
        begin, end = (min(K, (group + more) * rows_here) for more in (0, 1))
        spread.append(
            jnp.pad(subspace[begin:end], ((0, share * slab_count - (end - begin)), (0, 0)))
        )
    basis_part = lax.dot_general(
        subspace, jnp.concatenate(spread), across, preferred_element_type=jnp.float32
    ).T.astype(jnp.bfloat16)
    basis_part = basis_part.reshape(tuple(sizes) + (share, K))

    cells = jnp.pad(
        raw_frames.transpose(1, 0, 2), ((0, 0), (0, 0), (LEFT, SPAN - WIDE - LEFT))
    ).reshape(slab_depth * frames_here, -1)
    centered, basis_rows = smooth(
        cells, jnp.asarray(plane_weights()), weight_at, cell_at, basis_part,
        sizes, slab_depth, frames_here, extent, own, rim,
    )
    basis_rows = basis_rows.reshape(share * slab_count, K)[:rows_here].astype(jnp.float32)

    stacked = jnp.concatenate([subspace, centered], 0)
    data_part = lax.dot_general(
        stacked, centered, across, preferred_element_type=jnp.float32
    ).T.astype(jnp.bfloat16)
    flat = (1, group_count) + tuple(sizes[2:])
    data_part = data_part.reshape(flat + (-1, order_rows))
    data = sum_over_all(data_part, flat).reshape(frame_count, order_rows).astype(jnp.float32)
    row = lax.broadcasted_iota(jnp.int32, data.shape, 0)
    column = lax.broadcasted_iota(jnp.int32, data.shape, 1)
    squares = jnp.sum(jnp.where(row + K == column, data, 0.0), axis=1)
    power = jnp.sum(squares.reshape(2, subject_frames), axis=1)
    scales = lax.rsqrt(power / (masked * subject_frames) + epsilon)
    row_scale = jnp.concatenate([jnp.ones((K,), jnp.float32), jnp.repeat(scales, subject_frames)])

    turned = (rotation.astype(jnp.float32) * row_scale[:, None]).astype(jnp.bfloat16)
    new_subspace = lax.dot_general(
        turned, stacked, (((0,), (0,)), ((), ())), preferred_element_type=jnp.float32
    ).astype(jnp.bfloat16)

    right = lax.dynamic_slice_in_dim(data, first_row, rows_here, 1).T
    low = jnp.pad(data[:, :K], ((rows_here, rows_here), (0, 0)))
    low = lax.dynamic_slice_in_dim(low, jnp.maximum(first_row - K + rows_here, 0), rows_here, 0)
    owned = jnp.concatenate([basis_rows + low, right], 1)
    owned_scale = lax.dynamic_slice_in_dim(row_scale, first_row, rows_here, 0)
    gram_rows = owned * (owned_scale[:, None] * row_scale[None, :]) / masked
    return (gram_rows, new_subspace)


def solution(mesh):
    placed = (P("grp", "slab", None), P(("slab", "grp")), P(None, ("slab", "grp")), P())
    return jax.shard_map(
        body,
        mesh=mesh,
        in_specs=placed,
        out_specs=(P("grp", None), P(None, ("slab", "grp"))),
        check_vma=False,
    )
```

```python
import functools
import math

import jax
import jax.numpy as jnp
import numpy as np
from jax import lax
from jax.experimental import pallas as pl
from jax.experimental.pallas import tpu as pltpu
from jax.sharding import PartitionSpec as P

NX = 96
RUN = 128
RAD = 3
K = 1200
MESH = pl.DeviceIdType.MESH

smooth_sigma = 1.0617
epsilon = 1e-06

WIDE = 2 * RUN
LEFT = 3 * RUN
SPAN = 8 * RUN


def tap_weights():
    unscaled = [
        math.exp(-offset * offset / (2.0 * smooth_sigma * smooth_sigma))
        for offset in range(-RAD, RAD + 1)
    ]
    summed = sum(unscaled)
    return [weight / summed for weight in unscaled]


def plane_weights():
    taps = np.array(tap_weights())
    kinds = NX // math.gcd(WIDE, NX)
    out = np.zeros((kinds, SPAN, WIDE))
    for kind in range(kinds):
        target = np.arange(WIDE)
        column = (kind * WIDE + target) % NX
        for dy in range(-RAD, RAD + 1):
            for dx in range(-RAD, RAD + 1):
                inside = (column + dx >= 0) & (column + dx < NX)
                source = target + LEFT + dy * NX + dx
                out[kind, source[inside], target[inside]] = taps[dy + RAD] * taps[dx + RAD]
    return out.astype(jnp.bfloat16)


def exchange_kernel(total, groups, summed, x_ref, out_ref, landed, send_sem, recv_sem):
    me = lax.axis_index("slab") * groups + lax.axis_index("grp")
    barrier = pltpu.get_barrier_semaphore()

    def place(peer):
        return (peer // groups, lax.rem(peer, groups))

    def greet(step, _):
        pl.semaphore_signal(
            barrier, inc=1, device_id=place(lax.rem(me + step, total)), device_id_type=MESH
        )
        return 0

    lax.fori_loop(1, total, greet, 0)
    pl.semaphore_wait(barrier, total - 1)

    def copy(step):
        return pltpu.make_async_remote_copy(
            src_ref=x_ref,
            dst_ref=landed.at[step],
            send_sem=send_sem.at[step],
            recv_sem=recv_sem.at[step],
            device_id=place(lax.rem(me + step, total)),
            device_id_type=MESH,
        )

    def start(step, _):
        copy(step).start()
        return 0

    def finish(step, _):
        copy(step).wait()
        return 0

    lax.fori_loop(1, total, start, 0)
    landed[0] = x_ref[...]
    lax.fori_loop(1, total, finish, 0)
    if summed:
        out_ref[...] = jnp.sum(landed[...], axis=0)
    else:
        def put(step, _):
            out_ref[lax.rem(me + total - step, total)] = landed[step]
            return 0

        lax.fori_loop(0, total, put, 0)


def exchange(x, summed, collective_id):
    groups = lax.axis_size("grp")
    total = groups * lax.axis_size("slab")
    shape = x.shape if summed else (total,) + x.shape
    return pl.pallas_call(
        functools.partial(exchange_kernel, total, groups, summed),
        out_shape=jax.ShapeDtypeStruct(shape, x.dtype),
        in_specs=[pl.BlockSpec(memory_space=pltpu.VMEM)],
        out_specs=pl.BlockSpec(memory_space=pltpu.VMEM),
        scratch_shapes=[
            pltpu.VMEM((total,) + x.shape, x.dtype),
            pltpu.SemaphoreType.DMA((total,)),
            pltpu.SemaphoreType.DMA((total,)),
        ],
        compiler_params=pltpu.CompilerParams(
            collective_id=collective_id, has_side_effects=True
        ),
    )(x)


def axes_of(groups, slabs):
    outer = 4 if groups % 4 == 0 else 1
    cores = 2 if slabs % 2 == 0 else 1
    return outer, groups // outer, slabs // cores, cores


def coordinates(sizes):
    slab, grp = lax.axis_index("slab"), lax.axis_index("grp")
    return [grp // sizes[1], lax.rem(grp, sizes[1]), slab // sizes[3], lax.rem(slab, sizes[3])]


def device_at(at, sizes):
    return (at[2] * sizes[3] + at[3], at[0] * sizes[1] + at[1])


def moved(at, sizes, axis, step):
    other = lax.rem(at[axis] + step, sizes[axis])
    return at[:axis] + [other] + at[axis + 1 :], other


def greet_all(sizes):
    barrier = pltpu.get_barrier_semaphore()
    at = coordinates(sizes)
    count = 0
    for axis, size in enumerate(sizes):
        for step in range(1, size):
            there, _ = moved(at, sizes, axis, step)
            pl.semaphore_signal(
                barrier, inc=1, device_id=device_at(there, sizes), device_id_type=MESH
            )
            count += 1
    return barrier, count


class Scatter:
    def __init__(self, sizes, axis, left, src, landed, out, sems):
        self.sizes, self.axis, self.src, self.landed, self.out = sizes, axis, src, landed, out
        self.dim = left.index(axis)
        self.left = [other for other in left if other != axis]
        self.send_sem, self.recv_sem = sems
        self.at = coordinates(sizes)

    def part(self, where):
        return self.src.at[(slice(None),) * self.dim + (where,)]

    def copy(self, step):
        there, other = moved(self.at, self.sizes, self.axis, step)
        return pltpu.make_async_remote_copy(
            src_ref=self.part(other),
            dst_ref=self.landed.at[step - 1],
            send_sem=self.send_sem.at[self.axis, step],
            recv_sem=self.recv_sem.at[self.axis, step],
            device_id=device_at(there, self.sizes),
            device_id_type=MESH,
        )

    def start(self):
        for step in range(1, self.sizes[self.axis]):
            self.copy(step).start()

    def finish(self):
        for step in range(1, self.sizes[self.axis]):
            self.copy(step).wait()
        mine = self.part(self.at[self.axis])
        lead = [self.sizes[axis] for axis in self.left]
        total = math.prod(lead)

        def add(index, _):
            where = []
            for size in reversed(lead):
                where.insert(0, lax.rem(index, size))
                index = index // size
            where = tuple(where)
            value = mine[where].astype(jnp.float32)
            for step in range(self.sizes[self.axis] - 1):
                value = value + self.landed[(step,) + where].astype(jnp.float32)
            self.out[where] = value.astype(self.out.dtype)
            return 0

        lax.fori_loop(0, total, add, 0)


class Gather:
    def __init__(self, sizes, axis, full, first, sems):
        self.sizes, self.axis, self.full, self.first = sizes, axis, full, first
        self.send_sem, self.recv_sem = sems
        self.at = coordinates(sizes)

    def copy(self, step):
        there, _ = moved(self.at, self.sizes, self.axis, step)
        where = (slice(None),) * (self.axis - self.first) + tuple(self.at[self.axis :])
        return pltpu.make_async_remote_copy(
            src_ref=self.full.at[where],
            dst_ref=self.full.at[where],
            send_sem=self.send_sem.at[self.axis, step],
            recv_sem=self.recv_sem.at[self.axis, step],
            device_id=device_at(there, self.sizes),
            device_id_type=MESH,
        )

    def start(self):
        for step in range(1, self.sizes[self.axis]):
            self.copy(step).start()

    def finish(self):
        for step in range(1, self.sizes[self.axis]):
            self.copy(step).wait()


STAGES = (3, 1, 2, 0)


def stage_scratch(sizes, piece):
    out = []
    left = [axis for axis in range(4) if sizes[axis] > 1]
    for axis in STAGES:
        if sizes[axis] == 1:
            continue
        left.remove(axis)
        shape = tuple(sizes[other] for other in left) + piece
        out.append(pltpu.VMEM((sizes[axis] - 1,) + shape, jnp.bfloat16))
        if left:
            out.append(pltpu.VMEM(shape, jnp.bfloat16))
    return out


def stage_sems(sizes):
    most = max(sizes)
    return [pltpu.SemaphoreType.DMA((4, most)) for _ in range(4)]


def scatter_stages(sizes, src, bufs, result, sems):
    stages = []
    left = [0, 1, 2, 3]
    for axis in STAGES:
        if sizes[axis] == 1:
            src = src.at[(slice(None),) * left.index(axis) + (0,)]
            left = [other for other in left if other != axis]
    order = [axis for axis in STAGES if sizes[axis] > 1]
    for number, axis in enumerate(order):
        last = number == len(order) - 1
        out = result if last else bufs[2 * number + 1]
        stages.append(Scatter(sizes, axis, left, src, bufs[2 * number], out, sems))
        left = stages[-1].left
        src = out
    return stages


def smooth_kernel(sizes, depth, frames, own, rim, z_ref, r_ref, x_ref, w_ref, gram_ref,
                  out_ref, rows_ref, y_ref, full, up_ref, down_ref, below, above, picked_ref,
                  regrouped, halo_send, halo_recv, all_send, all_recv,
                  s_send, s_recv, g_send, g_recv, *bufs):
    kinds = w_ref.shape[0]
    steps = y_ref.shape[0] // (2 * kinds * depth)
    groups, slabs = sizes[0] * sizes[1], sizes[2] * sizes[3]
    slab, grp = lax.axis_index("slab"), lax.axis_index("grp")
    at = coordinates(sizes)
    runs = own // groups
    upper = lax.rem(slab + 1, slabs)
    lower = lax.rem(slab + slabs - 1, slabs)

    barrier, count = greet_all(sizes)
    for other in (upper, lower):
        pl.semaphore_signal(barrier, inc=1, device_id=(other, grp), device_id_type=MESH)
    for step in range(1, groups):
        pl.semaphore_signal(
            barrier, inc=1, device_id=(slab, lax.rem(grp + step, groups)), device_id_type=MESH
        )
    pl.semaphore_wait(barrier, count + 2 + groups - 1)

    scatter = scatter_stages(sizes, gram_ref, bufs, full.at[at[2], at[3]], (s_send, s_recv))
    gather = [Gather(sizes, axis, full, 2, (g_send, g_recv)) for axis in (2, 3)]

    def planar(step, _):
        for kind in range(kinds):
            place = step * kinds + kind
            begin = pl.multiple_of(place * WIDE, WIDE)
            found = jnp.dot(
                x_ref[:, pl.ds(begin, SPAN)], w_ref[kind], preferred_element_type=jnp.float32
            )
            for side in range(2):
                y_ref[pl.ds((2 * place + side) * depth, depth)] = found[
                    :, side * RUN : (side + 1) * RUN
                ].reshape(depth, frames, RUN)
        return 0

    def picked(run):
        total = None
        for tap in range(2 * RAD + 1):
            term = z_ref[run * (2 * RAD + 1) + tap] * y_ref[r_ref[run * (2 * RAD + 1) + tap]]
            total = term if total is None else total + term
        return total

    def put(ref, first):
        def one(run, _):
            ref[run] = picked(run + first).astype(ref.dtype)
            return 0

        lax.fori_loop(0, rim, one, 0)

    def halo(src, dst, number, other):
        return pltpu.make_async_remote_copy(
            src_ref=src, dst_ref=dst, send_sem=halo_send.at[number], recv_sem=halo_recv.at[number],
            device_id=(other, grp), device_id_type=MESH,
        )

    scatter[0].start()
    early = steps // 3
    lax.fori_loop(0, early, planar, 0)
    scatter[0].finish()
    scatter[1].start()
    lax.fori_loop(early, steps, planar, 0)

    put(up_ref, own)
    halo_up = halo(up_ref, below, 0, upper)
    halo_up.start()
    put(down_ref, own + rim)
    halo_down = halo(down_ref, above, 1, lower)
    halo_down.start()

    def inner(run, _):
        picked_ref[run] = picked(run).astype(picked_ref.dtype)
        return 0

    lax.fori_loop(rim, own - rim, inner, 0)

    def trade(step):
        other = lax.rem(grp + step, groups)
        return pltpu.make_async_remote_copy(
            src_ref=picked_ref.at[pl.ds(other * runs, runs)], dst_ref=regrouped.at[grp],
            send_sem=all_send.at[step], recv_sem=all_recv.at[step],
            device_id=(slab, other), device_id_type=MESH,
        )

    outer = -(-rim // runs)

    def start_trades(at_rim):
        for step in range(1, groups):
            other = lax.rem(grp + step, groups)
            inside = (other >= outer) & (other < groups - outer)
            pl.when(jnp.logical_not(inside) if at_rim else inside)(trade(step).start)

    start_trades(False)
    scatter[1].finish()
    scatter[2].start()
    halo_up.wait()
    halo_down.wait()
    low_part = jnp.where(slab > 0, 1.0, 0.0)
    high_part = jnp.where(slab < slabs - 1, 1.0, 0.0)

    def edge(run, _):
        picked_ref[run] = (picked(run) + low_part * below[run].astype(jnp.float32)).astype(
            picked_ref.dtype
        )
        last = run + own - rim
        picked_ref[last] = (picked(last) + high_part * above[run].astype(jnp.float32)).astype(
            picked_ref.dtype
        )
        return 0

    lax.fori_loop(0, rim, edge, 0)

    start_trades(True)
    regrouped[grp] = picked_ref[pl.ds(grp * runs, runs)]

    scatter[2].finish()
    scatter[3].start()
    scatter[3].finish()
    for stage in gather:
        stage.start()
        stage.finish()
    for step in range(1, groups):
        trade(step).wait()
    rows_ref[...] = full[...]

    half = groups // 2
    for run in range(runs):
        lanes = slice(run * RUN, (run + 1) * RUN)
        for subject in range(2):
            block = regrouped[subject * half : (subject + 1) * half, run].astype(jnp.float32)
            block = block.reshape(half * frames, RUN)
            mean = jnp.sum(block, axis=0, keepdims=True) * (1.0 / (half * frames))
            out_ref[subject * half * frames : (subject + 1) * half * frames, lanes] = (
                block - mean
            ).astype(out_ref.dtype)


def smooth(cells, weights, planes_at, runs_at, gram, sizes, depth, frames, extent, own, rim):
    vmem = pl.BlockSpec(memory_space=pltpu.VMEM)
    smem = pl.BlockSpec(memory_space=pltpu.SMEM)
    groups = sizes[0] * sizes[1]
    runs = own // groups
    piece = gram.shape[4:]
    rim_shape = pltpu.VMEM((rim, frames, RUN), jnp.bfloat16)
    return pl.pallas_call(
        functools.partial(smooth_kernel, sizes, depth, frames, own, rim),
        out_shape=(
            jax.ShapeDtypeStruct((groups * frames, runs * RUN), jnp.bfloat16),
            jax.ShapeDtypeStruct(tuple(sizes[2:]) + piece, jnp.bfloat16),
        ),
        in_specs=[smem, smem, vmem, vmem, vmem],
        out_specs=(vmem, vmem),
        scratch_shapes=[
            pltpu.VMEM((extent // RUN * depth, frames, RUN), jnp.float32),
            pltpu.VMEM(tuple(sizes[2:]) + piece, jnp.bfloat16),
            rim_shape, rim_shape, rim_shape, rim_shape,
            pltpu.VMEM((own, frames, RUN), jnp.bfloat16),
            pltpu.VMEM((groups, runs, frames, RUN), jnp.bfloat16),
            pltpu.SemaphoreType.DMA((2,)),
            pltpu.SemaphoreType.DMA((2,)),
            pltpu.SemaphoreType.DMA((groups,)),
            pltpu.SemaphoreType.DMA((groups,)),
        ]
        + stage_sems(sizes)
        + stage_scratch(sizes, piece),
        compiler_params=pltpu.CompilerParams(
            collective_id=2, has_side_effects=True, vmem_limit_bytes=60 * 1024 * 1024
        ),
    )(planes_at, runs_at, cells, weights, gram)


def sum_kernel(sizes, part_ref, out_ref, full, s_send, s_recv, g_send, g_recv, *bufs):
    at = coordinates(sizes)
    barrier, count = greet_all(sizes)
    pl.semaphore_wait(barrier, count)
    for stage in scatter_stages(sizes, part_ref, bufs, full.at[tuple(at)], (s_send, s_recv)):
        stage.start()
        stage.finish()
    for axis in range(4):
        stage = Gather(sizes, axis, full, 0, (g_send, g_recv))
        stage.start()
        stage.finish()
    out_ref[...] = full[...]


def sum_over_all(part, sizes):
    piece = part.shape[4:]
    vmem = pl.BlockSpec(memory_space=pltpu.VMEM)
    return pl.pallas_call(
        functools.partial(sum_kernel, sizes),
        out_shape=jax.ShapeDtypeStruct(part.shape, part.dtype),
        in_specs=[vmem],
        out_specs=vmem,
        scratch_shapes=[pltpu.VMEM(part.shape, part.dtype)]
        + stage_sems(sizes)
        + stage_scratch(sizes, piece),
        compiler_params=pltpu.CompilerParams(collective_id=3, has_side_effects=True),
    )(part)


def body(raw_frames, mask_index, subspace, rotation):
    frames_here, slab_depth, extent = raw_frames.shape
    per_device = subspace.shape[1]
    group_count = lax.axis_size("grp")
    slab_count = lax.axis_size("slab")
    sizes = axes_of(group_count, slab_count)
    masked = per_device * slab_count * group_count
    frame_count = frames_here * group_count
    subject_frames = frame_count // 2
    order_rows = K + frame_count
    rows_here = order_rows // group_count
    first_row = lax.axis_index("grp") * rows_here
    slab = lax.axis_index("slab")
    runs_here = per_device // RUN
    own = runs_here * group_count
    rim = own * RAD // slab_depth
    across = (((1,), (1,)), ((), ()))

    starts = jnp.pad(mask_index.reshape(runs_here, RUN)[:, 0], (0, RUN - runs_here))
    starts = exchange(starts.reshape(1, RUN), False, 1)[:, 0, :runs_here]
    starts = starts.reshape(slab_count, own) - slab * (slab_depth * extent)
    wanted = jnp.concatenate(
        [
            lax.dynamic_index_in_dim(starts, slab, 0, False),
            lax.dynamic_index_in_dim(starts, jnp.minimum(slab + 1, slab_count - 1), 0, False)[:rim],
            lax.dynamic_index_in_dim(starts, jnp.maximum(slab - 1, 0), 0, False)[own - rim :],
        ]
    )
    planes_at = jnp.floor_divide(wanted, extent)
    runs_at = (wanted - planes_at * extent) // RUN
    planes = planes_at[:, None] + jnp.arange(-RAD, RAD + 1, dtype=jnp.int32)[None, :]
    taps = jnp.asarray(tap_weights(), jnp.float32)[None, :]
    weight_at = jnp.where((planes >= 0) & (planes < slab_depth), taps, 0.0).reshape(-1)
    cell_at = runs_at[:, None] * slab_depth + jnp.clip(planes, 0, slab_depth - 1)
    cell_at = cell_at.reshape(-1)

    share = -(-rows_here // (16 * slab_count)) * 16
    spread = []
    for group in range(group_count):
        begin, end = (min(K, (group + more) * rows_here) for more in (0, 1))
        spread.append(
            jnp.pad(subspace[begin:end], ((0, share * slab_count - (end - begin)), (0, 0)))
        )
    basis_part = lax.dot_general(
        subspace, jnp.concatenate(spread), across, preferred_element_type=jnp.float32
    ).T.astype(jnp.bfloat16)
    basis_part = basis_part.reshape(tuple(sizes) + (share, K))

    cells = jnp.pad(
        raw_frames.transpose(1, 0, 2), ((0, 0), (0, 0), (LEFT, SPAN - WIDE - LEFT))
    ).reshape(slab_depth * frames_here, -1)
    centered, basis_rows = smooth(
        cells, jnp.asarray(plane_weights()), weight_at, cell_at, basis_part,
        sizes, slab_depth, frames_here, extent, own, rim,
    )
    basis_rows = basis_rows.reshape(share * slab_count, K)[:rows_here].astype(jnp.float32)

    stacked = jnp.concatenate([subspace, centered], 0)
    data_part = lax.dot_general(
        stacked, centered, across, preferred_element_type=jnp.float32
    ).T.astype(jnp.bfloat16)
    flat = (1, group_count) + tuple(sizes[2:])
    data_part = data_part.reshape(flat + (-1, order_rows))
    data = sum_over_all(data_part, flat).reshape(frame_count, order_rows).astype(jnp.float32)
    row = lax.broadcasted_iota(jnp.int32, data.shape, 0)
    column = lax.broadcasted_iota(jnp.int32, data.shape, 1)
    squares = jnp.sum(jnp.where(row + K == column, data, 0.0), axis=1)
    power = jnp.sum(squares.reshape(2, subject_frames), axis=1)
    scales = lax.rsqrt(power / (masked * subject_frames) + epsilon)
    row_scale = jnp.concatenate([jnp.ones((K,), jnp.float32), jnp.repeat(scales, subject_frames)])

    turned = (rotation.astype(jnp.float32) * row_scale[:, None]).astype(jnp.bfloat16)
    new_subspace = lax.dot_general(
        turned, stacked, (((0,), (0,)), ((), ())), preferred_element_type=jnp.float32
    ).astype(jnp.bfloat16)

    right = lax.dynamic_slice_in_dim(data, first_row, rows_here, 1).T
    low = jnp.pad(data[:, :K], ((rows_here, rows_here), (0, 0)))
    low = lax.dynamic_slice_in_dim(low, jnp.maximum(first_row - K + rows_here, 0), rows_here, 0)
    owned = jnp.concatenate([basis_rows + low, right], 1)
    owned_scale = lax.dynamic_slice_in_dim(row_scale, first_row, rows_here, 0)
    gram_rows = owned * (owned_scale[:, None] * row_scale[None, :]) / masked
    return (gram_rows, new_subspace)


def solution(mesh):
    placed = (P("grp", "slab", None), P(("slab", "grp")), P(None, ("slab", "grp")), P())
    return jax.shard_map(
        body,
        mesh=mesh,
        in_specs=placed,
        out_specs=(P("grp", None), P(None, ("slab", "grp"))),
        check_vma=False,
    )
```
